32 devices in a mesh: gx: 4 (over y, core), gy: 2 (over x), gz: 4 (over z).
Axes of the slice: x: 2, y: 2, z: 4, core: 2. Of those that a mesh axis runs over, the one named last changes fastest.
Arguments:
- features: bfloat16 [8, 2, 16, 128, 128], P('gx', 'gy', 'gz'), may hold values from -6 to 6
- msg_weight: bfloat16 [128, 128], replicated, may hold values from -0.5 to 0.5
- self_weight: bfloat16 [128, 128], replicated, may hold values from -0.5 to 0.5
- charge_weight: bfloat16 [128], replicated, may hold values from -0.5 to 0.5
- spline_corner: int32 [8, 2, 16, 3, 128], P('gx', 'gy', 'gz'), may hold values from 0 to 12
- spline_fraction: float32 [8, 2, 16, 3, 128], P('gx', 'gy', 'gz'), may hold values from 0 to 1
Outputs:
- feature_grad: float32 [8, 2, 16, 128, 128], P('gx', 'gy', 'gz')
- atom_potential: float32 [8, 2, 16, 128], P('gx', 'gy', 'gz')
- energy_per_atom: float32 [], replicated
The draws below stay inside these ranges and needn't reach their ends.
All inputs are finite; a program needn't handle non-finite values.
Results may differ from the reference program's by a relative error of at most 0.0095.
Values may be sent and summed in bfloat16 or wider, within the bound.
A program may use at most 64 MiB of HBM per device.

```python
import math
import jax
import jax.numpy as jnp
from jax import lax

D = 128
M = 128
PC = 16
NCX = 8
NCY = 2
NCZ = 16
NX = 128
NY = 32
NZ = 256


def set_ends(values, own_key, least, top_value):
    longest = values.shape.index(max(values.shape))
    spots = []
    for shift in (0, 1):
        where = [jax.random.randint(jax.random.fold_in(own_key, axis), (), 0, length) for axis, length in enumerate(values.shape)]
        where[longest] = (where[longest] + shift) % values.shape[longest]
        spots.append(tuple(where))
    return values.at[spots[0]].set(least).at[spots[1]].set(top_value)


def level_of(key, extent, split, low, high):
    def one(axis_at, shards_of):
        draws = jax.random.uniform(jax.random.fold_in(jax.random.fold_in(key, 6), axis_at), (shards_of,), jnp.float32, low / len(split), high / len(split))
        return jnp.repeat(jnp.exp(draws), extent[axis_at] // shards_of).reshape((-1,) + (1,) * (len(extent) - axis_at - 1))

    gain = one(*split[0])
    for cut in split[1:]:
        gain = gain * one(*cut)
    return gain


def gaussian(stream_key, shape, deviation, most, split=(), kind=jnp.bfloat16):
    values = jax.random.normal(stream_key, shape, jnp.float32) * deviation
    if len(split) > 0:
        values = level_of(stream_key, shape, split, -0.22, 0.18) * values
    return jnp.clip(values, min=-most, max=most).astype(kind)


def setup_inputs(seed: int = 0) -> dict:
    key_list = jax.random.split(jax.random.key(seed), 7)
    return {
        "features": gaussian(key_list[0], (NCX, NCY, NCZ, M, D), 1.0, 6.0, ((0, 4), (1, 2), (2, 4))),
        "msg_weight": gaussian(key_list[1], (D, D), D ** -0.5, 0.5),
        "self_weight": gaussian(key_list[2], (D, D), D ** -0.5, 0.5),
        "charge_weight": gaussian(key_list[3], (D,), D ** -0.5, 0.5),
        "spline_corner": set_ends(jax.random.randint(key_list[4], (NCX, NCY, NCZ, 3, M), 0, PC - 3), jax.random.fold_in(key_list[4], 1), 0, (PC - 3) - 1).astype(jnp.int32),
        "spline_fraction": jnp.clip(1.0 * jax.random.uniform(key_list[5], (NCX, NCY, NCZ, 3, M), jnp.float32) ** level_of(key_list[5], (NCX, NCY, NCZ, 3, M), ((0, 4), (1, 2), (2, 4)), -0.2, 0.2), 0.0, 1.0),
    }


pair_scale = 0.1
coupling = 0.125
spread_width = 0.0625
highest = lax.Precision.HIGHEST


def spline_rows(corner, fraction, mesh_points):
    offset = jnp.arange(mesh_points, dtype=jnp.int32) - corner[..., None]
    within = fraction[..., None]
    first_weight = (1.0 - within) ** 3 / 6.0
    second_weight = (3.0 * within ** 3 - 6.0 * within ** 2 + 4.0) / 6.0
    third_weight = (-3.0 * within ** 3 + 3.0 * within ** 2 + 3.0 * within + 1.0) / 6.0
    fourth_weight = within ** 3 / 6.0
    nothing = jnp.zeros_like(first_weight)
    return jnp.where(offset == 0, first_weight, jnp.where(offset == 1, second_weight, jnp.where(offset == 2, third_weight, jnp.where(offset == 3, fourth_weight, nothing))))


def pair_weights(centre, neighbour, offset):
    centre = centre.astype(jnp.float32)
    neighbour = neighbour.astype(jnp.float32)
    squared = None
    for which in range(3):
        gap = offset[which] + (neighbour[..., which, None, :] - centre[..., which, :, None])
        squared = gap * gap if squared is None else squared + gap * gap
    inside = jnp.maximum(1.0 - squared, 0.0)
    return (pair_scale * inside * inside).astype(jnp.bfloat16)


def all_offsets():
    return [(first, second, third) for first in (-1, 0, 1) for second in (-1, 0, 1) for third in (-1, 0, 1)]


def pair_sums(position, values):
    total = jnp.zeros(values.shape, jnp.float32)
    for offset in all_offsets():
        moved = (-offset[0], -offset[1], -offset[2])
        near_position = jnp.roll(position, moved, axis=(0, 1, 2))
        near_values = jnp.roll(values, moved, axis=(0, 1, 2))
        weights = pair_weights(position, near_position, offset)
        total = total + jnp.einsum('abcsn,abcnd->abcsd', weights.astype(jnp.float32), near_values.astype(jnp.float32))
    return total


def spread_cells(charge, rows):
    points = rows[0].shape[-1]
    left = charge[..., None] * rows[0]
    right = (rows[1][..., :, None] * rows[2][..., None, :]).reshape(rows[1].shape[:-1] + (points * points,))
    block = jnp.einsum('abcsi,abcsj->abcij', left, right, precision=highest)
    return block.reshape(block.shape[:-1] + (points, points))


def interpolate(cell_field, rows):
    points = rows[0].shape[-1]
    right = (rows[1][..., :, None] * rows[2][..., None, :]).reshape(rows[1].shape[:-1] + (points * points,))
    flat_field = cell_field.reshape(cell_field.shape[:3] + (points, points * points))
    partial_value = jnp.einsum('abcij,abcsj->abcsi', flat_field, right, precision=highest)
    return jnp.sum(partial_value * rows[0], axis=-1)


def cells_to_mesh(block):
    count_a, count_b, count_c, points = block.shape[0], block.shape[1], block.shape[2], block.shape[3]
    return block.transpose(0, 3, 1, 4, 2, 5).reshape(count_a * points, count_b * points, count_c * points)


def mesh_to_cells(field, count_a, count_b, count_c):
    points = field.shape[0] // count_a
    return field.reshape(count_a, points, count_b, points, count_c, points).transpose(0, 2, 4, 1, 3, 5)


def influence_of(index_x, index_y, index_z, size_x, size_y, size_z, points):
    def wave(index, size):
        signed = jnp.where(2 * index >= size, index - size, index)
        return signed.astype(jnp.float32) * (points / size)
    wave_x = wave(index_x, size_x)
    wave_y = wave(index_y, size_y)
    wave_z = wave(index_z, size_z)
    squared = wave_x * wave_x + wave_y * wave_y + wave_z * wave_z
    safe = jnp.where(squared > 0, squared, 1.0)
    return jnp.where(squared > 0, jnp.exp(-(math.pi * spread_width) ** 2 * squared) / safe, 0.0)


def reference(features, msg_weight, self_weight, charge_weight, spline_corner, spline_fraction):
    width = features.shape[-1]
    position = ((spline_corner.astype(jnp.float32) + 1.0 + spline_fraction) / PC).astype(jnp.bfloat16)
    flat = features.reshape(-1, width)
    projected = jnp.dot(flat, msg_weight, preferred_element_type=jnp.float32).astype(jnp.bfloat16).reshape(features.shape)
    message = pair_sums(position, projected)
    preact = jnp.dot(flat, self_weight, preferred_element_type=jnp.float32).reshape(features.shape) + message
    charge = jnp.sum(jax.nn.silu(preact) * charge_weight.astype(jnp.float32), axis=-1)
    rows = [spline_rows(spline_corner[..., which, :], spline_fraction[..., which, :], PC) for which in range(3)]
    mesh = cells_to_mesh(spread_cells(charge, rows))
    spectrum = jnp.fft.fftn(mesh)
    grid_x = jnp.arange(NX, dtype=jnp.int32)[:, None, None]
    grid_y = jnp.arange(NY, dtype=jnp.int32)[None, :, None]
    grid_z = jnp.arange(NZ, dtype=jnp.int32)[None, None, :]
    influence = influence_of(grid_x, grid_y, grid_z, NX, NY, NZ, PC)
    volume = (NX // PC) * (NY // PC) * (NZ // PC)
    natoms = NCX * NCY * NCZ * M
    power = jnp.real(spectrum) ** 2 + jnp.imag(spectrum) ** 2
    energy = (coupling / (2.0 * volume * natoms)) * jnp.sum(influence * power)
    mesh_potential = ((coupling / volume) * (NX * NY * NZ) * jnp.real(jnp.fft.ifftn(influence * spectrum))).astype(jnp.float32)
    atom_potential = interpolate(mesh_to_cells(mesh_potential, NCX, NCY, NCZ), rows)
    sigma = jax.nn.sigmoid(preact)
    slope = sigma * (1.0 + preact * (1.0 - sigma))
    cotangent = (atom_potential[..., None] * charge_weight.astype(jnp.float32) * slope).astype(jnp.bfloat16)
    back_message = pair_sums(position, cotangent).astype(jnp.bfloat16)
    grad = jnp.dot(back_message.reshape(-1, width), msg_weight.T, preferred_element_type=jnp.float32)
    grad = grad + jnp.dot(cotangent.reshape(-1, width), self_weight.T, preferred_element_type=jnp.float32)
    return grad.reshape(features.shape), atom_potential, energy.astype(jnp.float32)
```

```python
import functools
import math

import jax
import jax.numpy as jnp
from jax import lax
from jax.experimental import pallas as pl
from jax.experimental.pallas import tpu as pltpu
from jax.sharding import PartitionSpec as P

PC = 16
LANES = 128
pair_scale = 0.1
coupling = 0.125
spread_width = 0.0625
highest = lax.Precision.HIGHEST
AXES = ("gx", "gy", "gz")
f32 = jnp.float32
bf16 = jnp.bfloat16
NT = (((1,), (1,)), ((), ()))
TN = (((0,), (0,)), ((), ()))


def full_spec(shape):
    return pl.BlockSpec(shape, lambda *_: (0,) * len(shape))


def cell_spec(shape):
    return pl.BlockSpec((1,) + tuple(shape[1:]), lambda i: (i,) + (0,) * (len(shape) - 1))


def split3(value):
    hi = lax.reduce_precision(value, 8, 7)
    rest = value - hi
    mid = lax.reduce_precision(rest, 8, 7)
    return hi, mid, rest - mid


def cas(first, second, length):
    angle = 2.0 * math.pi / length * (first[:, None] * second[None, :] % length).astype(f32)
    return jnp.cos(angle) + jnp.sin(angle)


def offsets():
    return [(i, j, k) for i in (-1, 0, 1) for j in (-1, 0, 1) for k in (-1, 0, 1)]


def offset_table():
    rows = []
    for o in offsets():
        norm = float(o[0] ** 2 + o[1] ** 2 + o[2] ** 2)
        doubled = [2.0 * v for v in o]
        rows.append([1.0] * 6 + doubled + [1.0] * 3 + [-v for v in doubled] + [-norm])
    return jnp.broadcast_to(jnp.array(rows, f32)[:, :, None], (27, 16, LANES)).astype(bf16)


def slot(offset, devices, length):
    if devices == 2 and length == 1:
        return 0 if offset == 0 else 1
    return 1 + offset


def with_halo(shard, axis, dim):
    devices, length = lax.axis_size(axis), shard.shape[dim]
    up = [(i, (i + 1) % devices) for i in range(devices)]
    down = [(j, i) for i, j in up]
    if devices == 2 and length == 1:
        return jnp.concatenate([shard, lax.ppermute(shard, axis, up)], axis=dim)
    last = lax.slice_in_dim(shard, length - 1, length, axis=dim)
    first = lax.slice_in_dim(shard, 0, 1, axis=dim)
    before = lax.ppermute(last, axis, up)
    after = lax.ppermute(first, axis, down)
    return jnp.concatenate([before, shard, after], axis=dim)


def exchange_halo(shard):
    shard = with_halo(shard, "gy", 1)
    shard = with_halo(shard, "gx", 0)
    return with_halo(shard, "gz", 2)


def pair_total(cells, counts, centre, table_ref, near_ref, value_ref):
    index = pl.program_id(0)
    at_z = index % cells[2]
    at_y = index // cells[2] % cells[1]
    at_x = index // (cells[2] * cells[1])
    total = jnp.zeros((centre.shape[1], value_ref.shape[-1]), f32)
    for which, o in enumerate(offsets()):
        where = [
            base + slot(step, count, length)
            for base, step, count, length in zip((at_x, at_y, at_z), o, counts, cells)
        ]
        near = near_ref[where[0], where[1], where[2]] * table_ref[which]
        inside = lax.dot_general(centre, near, TN, preferred_element_type=f32)
        inside = jnp.maximum(inside, 0.0)
        weight = (pair_scale * inside * inside).astype(bf16)
        total = total + jnp.dot(
            weight, value_ref[where[0], where[1], where[2]], preferred_element_type=f32
        )
    return total


def message_kernel(
    cells, counts, centre_ref, table_ref, near_ref, value_ref, feature_ref, self_ref, read_ref, pre_ref, charge_ref
):
    message = pair_total(cells, counts, centre_ref[0], table_ref, near_ref, value_ref)
    preact = jnp.dot(feature_ref[0], self_ref[...], preferred_element_type=f32) + message
    pre_ref[0] = preact
    active = preact / (1.0 + jnp.exp(-preact))
    charge_ref[0] = lax.dot_general(
        read_ref[...], active, NT, precision=highest, preferred_element_type=f32
    )


def back_kernel(
    cells, counts, centre_ref, table_ref, near_ref, value_ref, cot_ref, msg_ref, self_ref, out_ref
):
    total = pair_total(cells, counts, centre_ref[0], table_ref, near_ref, value_ref)
    grad = lax.dot_general(total.astype(bf16), msg_ref[...], NT, preferred_element_type=f32)
    out_ref[0] = grad + lax.dot_general(
        cot_ref[0], self_ref[...], NT, preferred_element_type=f32
    )


def spline(corner, fraction, points, start=0):
    atoms = corner.shape[-1]
    offset = lax.broadcasted_iota(jnp.int32, (points, atoms), 0) - start - corner
    u = fraction
    first = (1.0 - u) * (1.0 - u) * (1.0 - u) / 6.0
    second = (3.0 * u * u * u - 6.0 * u * u + 4.0) / 6.0
    third = (-3.0 * u * u * u + 3.0 * u * u + 3.0 * u + 1.0) / 6.0
    fourth = u * u * u / 6.0
    zero = jnp.zeros((points, atoms), f32)
    return jnp.where(
        offset == 0,
        first,
        jnp.where(offset == 1, second, jnp.where(offset == 2, third, jnp.where(offset == 3, fourth, zero))),
    )


def spread_kernel(dims, corner_ref, fraction_ref, charge_ref, wave_ref, out_ref, hx_ref, left_ref):
    local_x, local_y, local_z, pack = dims
    rows_x = spline(corner_ref[0:1, :], fraction_ref[0:1, :], local_x)
    rows_y = spline(corner_ref[1:2, :], fraction_ref[1:2, :], local_y)
    hx_ref[...] = charge_ref[...] * jnp.dot(
        wave_ref[...], rows_x, precision=highest, preferred_element_type=f32
    )
    half = hx_ref.shape[0] // pack
    total = None
    for h in range(pack):

        def fill(k, carry):
            left_ref[pl.ds(pl.multiple_of(k * local_y, local_y), local_y), :] = (
                hx_ref[pl.ds(h * half + k, 1), :] * rows_y
            ).astype(bf16)
            return carry

        lax.fori_loop(0, half, fill, 0, unroll=8)
        right = spline(corner_ref[2:3, :], fraction_ref[2:3, :], LANES, h * local_z).astype(bf16)
        part = lax.dot_general(left_ref[...], right, NT, preferred_element_type=f32)
        total = part if total is None else total + part
    out_ref[...] = total.astype(bf16)


def plane_kernel(dims, count_x, got_ref, z_ref, y_ref, g_ref, out_ref):
    count_y, count_z, pack = dims
    rows = got_ref.shape[1]
    each = count_y * count_z
    halves = [None] * pack
    for c in range(count_z):
        stack = []
        for b in range(count_y):
            block = got_ref[b * count_z + c].astype(f32)
            for a in range(1, count_x):
                block = block + got_ref[a * each + b * count_z + c].astype(f32)
            stack.append(block)
        stack = jnp.concatenate(stack, axis=0)
        for h in range(pack):
            part = jnp.dot(stack, z_ref[c, h], precision=highest, preferred_element_type=f32)
            halves[h] = part if halves[h] is None else halves[h] + part
    lines = jnp.concatenate(halves, axis=0)
    wave = jnp.dot(y_ref[...], lines, precision=highest, preferred_element_type=f32)
    scaled = g_ref[...] * wave
    energy = jnp.sum(jnp.sum(scaled * wave, axis=1, keepdims=True), axis=0, keepdims=True)
    hi = energy.astype(bf16).astype(f32)
    mid = (energy - hi).astype(bf16).astype(f32)
    low = energy - hi - mid
    which = lax.broadcasted_iota(jnp.int32, (16, LANES), 0)
    tail = jnp.where(which == 0, hi, jnp.where(which == 1, mid, jnp.where(which == 2, low, 0.0)))
    back = lax.dot_general(y_ref[...], scaled, TN, precision=highest, preferred_element_type=f32)
    high = back.shape[0] // pack
    for c in range(count_z):
        total = None
        for h in range(pack):
            part = lax.dot_general(
                back[h * high : (h + 1) * high], z_ref[c, h], NT, precision=highest, preferred_element_type=f32
            )
            total = part if total is None else total + part
        for b in range(count_y):
            out_ref[b * count_z + c, 0:rows, :] = total[b * rows : (b + 1) * rows].astype(bf16)
            out_ref[b * count_z + c, rows : rows + 16, :] = tail.astype(bf16)


def field_kernel(dims, scale, escale, owners, corner_ref, fraction_ref, wave_ref, got_ref, out_ref, energy_ref, hx_ref):
    local_x, local_y, local_z, pack, rows = dims
    atoms = corner_ref.shape[-1]
    rows_x = spline(corner_ref[0:1, :], fraction_ref[0:1, :], local_x)
    rows_y = spline(corner_ref[1:2, :], fraction_ref[1:2, :], local_y)
    hx_ref[...] = jnp.dot(wave_ref[...], rows_x, precision=highest, preferred_element_type=f32)
    half = hx_ref.shape[0] // pack
    per = rows // local_y
    acc = jnp.zeros((local_y, atoms), f32)
    for h in range(pack):
        right = spline(corner_ref[2:3, :], fraction_ref[2:3, :], LANES, h * local_z).astype(bf16)

        def step(q, acc):
            block = got_ref[q, 0:rows, :]
            value = jnp.dot(block, right, preferred_element_type=f32)
            for k in range(per):
                acc = acc + value[k * local_y : (k + 1) * local_y] * hx_ref[
                    pl.ds(h * half + q * per + k, 1), :
                ]
            return acc

        acc = lax.fori_loop(0, owners, step, acc, unroll=4)
    value = scale * jnp.sum(acc * rows_y, axis=0, keepdims=True)
    out_ref[...] = jnp.broadcast_to(value, out_ref.shape)
    tail = jnp.zeros((16, LANES), f32)
    for q in range(owners):
        tail = tail + got_ref[q, rows : rows + 16, :].astype(f32)
    energy_ref[...] = jnp.broadcast_to(escale * jnp.sum(tail, axis=0, keepdims=True), energy_ref.shape)


def influence_of(index_x, index_y, index_z, size_x, size_y, size_z, points):
    def wave(index, size):
        signed = jnp.where(2 * index >= size, index - size, index)
        return signed.astype(f32) * (points / size)

    wave_x = wave(index_x, size_x)
    wave_y = wave(index_y, size_y)
    wave_z = wave(index_z, size_z)
    squared = wave_x * wave_x + wave_y * wave_y + wave_z * wave_z
    safe = jnp.where(squared > 0, squared, 1.0)
    return jnp.where(squared > 0, jnp.exp(-((math.pi * spread_width) ** 2) * squared) / safe, 0.0)


def exchange_planes(payload):
    return lax.all_to_all(payload, AXES, split_axis=0, concat_axis=0, tiled=True)


def params(**kw):
    return pltpu.CompilerParams(vmem_limit_bytes=48 * 1024 * 1024, **kw)


def body(features, msg_weight, self_weight, charge_weight, spline_corner, spline_fraction):
    cells = features.shape[:3]
    slots, width = features.shape[3:]
    number = cells[0] * cells[1] * cells[2]
    counts = tuple(lax.axis_size(a) for a in AXES)
    devices = counts[0] * counts[1] * counts[2]
    local = tuple(c * PC for c in cells)
    size = tuple(c * n for c, n in zip(local, counts))
    pack = LANES // local[2]
    planes = max(pack, size[0] // devices)
    owners = size[0] // planes
    inner = planes // pack
    rows = inner * local[1]
    atoms = number * slots
    volume = size[0] // PC * (size[1] // PC) * (size[2] // PC)

    flat = features.reshape(number * slots, width)
    projected = jnp.dot(flat, msg_weight, preferred_element_type=f32).astype(bf16).reshape(features.shape)
    position = lax.reduce_precision(
        (spline_corner.astype(f32) + 1.0 + spline_fraction) / PC, 8, 7
    )
    norm = jnp.sum(position * position, axis=3, keepdims=True)
    one = jnp.ones_like(norm)
    near = jnp.concatenate(
        [position, one, one, one, one, one, one, *split3(-norm), position, one], axis=3
    ).astype(bf16)
    centre = jnp.concatenate(
        [2.0 * position, *split3(1.0 - norm), position] + [one] * 7, axis=3
    ).astype(bf16).reshape(number, 16, slots)
    table = offset_table()

    padded = exchange_halo(jnp.concatenate([projected, near], axis=3))
    values = padded[:, :, :, :slots]
    nears = padded[:, :, :, slots:]

    read = jnp.broadcast_to(charge_weight.astype(f32)[None, :], (8, width))
    cell_features = features.reshape(number, slots, width)
    square = (number, slots, width)
    preact, charge = pl.pallas_call(
        functools.partial(message_kernel, cells, counts),
        out_shape=(jax.ShapeDtypeStruct(square, f32), jax.ShapeDtypeStruct((number, 8, slots), f32)),
        grid=(number,),
        in_specs=[
            cell_spec(centre.shape),
            full_spec(table.shape),
            full_spec(nears.shape),
            full_spec(values.shape),
            cell_spec(square),
            full_spec(self_weight.shape),
            full_spec(read.shape),
        ],
        out_specs=(cell_spec(square), cell_spec((number, 8, slots))),
        compiler_params=params(),
        name="message",
    )(centre, table, nears, values, cell_features, self_weight, read)

    shift = jnp.stack(
        [lax.broadcasted_iota(jnp.int32, cells + (slots,), d) * PC for d in range(3)], axis=0
    )
    corner = (spline_corner.transpose(3, 0, 1, 2, 4) + shift).reshape(3, atoms)
    fraction = spline_fraction.transpose(3, 0, 1, 2, 4).reshape(3, atoms)
    order = (
        jnp.arange(pack, dtype=jnp.int32)[:, None, None] * inner
        + jnp.arange(owners, dtype=jnp.int32)[None, :, None] * planes
        + jnp.arange(inner, dtype=jnp.int32)[None, None, :]
    ).reshape(-1)
    here = lax.axis_index("gx") * local[0] + jnp.arange(local[0], dtype=jnp.int32)
    wave_x = cas(order, here, size[0])
    charges = charge[:, 0, :].reshape(1, atoms)
    payload = pl.pallas_call(
        functools.partial(spread_kernel, (local[0], local[1], local[2], pack)),
        out_shape=jax.ShapeDtypeStruct((owners * rows, LANES), bf16),
        scratch_shapes=[
            pltpu.VMEM((size[0], atoms), f32),
            pltpu.VMEM((owners * rows, atoms), bf16),
        ],
        compiler_params=params(),
        name="spread",
    )(corner, fraction, charges, wave_x).reshape(owners, rows, LANES)
    if owners < devices:
        payload = jnp.pad(payload, ((0, devices - owners), (0, 0), (0, 0)))
    got = exchange_planes(payload)

    range_y = jnp.arange(size[1], dtype=jnp.int32)
    range_z = jnp.arange(size[2], dtype=jnp.int32)
    cas_z = cas(range_z, range_z, size[2]).reshape(counts[2], 1, local[2], size[2])
    blank = jnp.zeros_like(cas_z)
    wide_z = jnp.concatenate(
        [
            jnp.concatenate([cas_z if at == h else blank for at in range(pack)], axis=2)
            for h in range(pack)
        ],
        axis=1,
    )
    cas_y = cas(range_y, range_y, size[1]).reshape(size[1], counts[1], local[1])
    same = jnp.eye(planes, dtype=f32).reshape(pack, inner, pack, inner)
    wide_y = jnp.einsum("abcd,kgy->abkcgdy", same, cas_y, precision=highest).reshape(
        planes * size[1], planes * size[1]
    )
    me = lax.axis_index(AXES)
    index_x = me * planes + jnp.arange(planes, dtype=jnp.int32)
    influence = influence_of(
        index_x[:, None, None], range_y[None, :, None], range_z[None, None, :], *size, PC
    ).reshape(planes * size[1], size[2])
    each = counts[1] * counts[2]
    solved = pl.pallas_call(
        functools.partial(plane_kernel, (counts[1], counts[2], pack), counts[0]),
        out_shape=jax.ShapeDtypeStruct((each, rows + 16, LANES), bf16),
        compiler_params=params(),
        name="planes",
    )(got, wide_z, wide_y, influence)
    field = exchange_planes(jnp.tile(solved, (counts[0], 1, 1)))

    potential, energy = pl.pallas_call(
        functools.partial(
            field_kernel,
            (local[0], local[1], local[2], pack, rows),
            coupling / volume,
            coupling / (2.0 * volume * atoms * devices),
            owners,
        ),
        out_shape=(jax.ShapeDtypeStruct((8, atoms), f32), jax.ShapeDtypeStruct((8, LANES), f32)),
        scratch_shapes=[pltpu.VMEM((size[0], atoms), f32)],
        compiler_params=params(),
        name="field",
    )(corner, fraction, wave_x, field)
    potential = potential[0].reshape(cells + (slots,))

    pre = preact.reshape(features.shape)
    sigma = jax.nn.sigmoid(pre)
    slope = sigma * (1.0 + pre * (1.0 - sigma))
    cotangent = (potential[..., None] * charge_weight.astype(f32) * slope).astype(bf16)
    cots = exchange_halo(cotangent)
    grad = pl.pallas_call(
        functools.partial(back_kernel, cells, counts),
        out_shape=jax.ShapeDtypeStruct(square, f32),
        grid=(number,),
        in_specs=[
            cell_spec(centre.shape),
            full_spec(table.shape),
            full_spec(nears.shape),
            full_spec(cots.shape),
            cell_spec(square),
            full_spec(msg_weight.shape),
            full_spec(self_weight.shape),
        ],
        out_specs=cell_spec(square),
        compiler_params=params(),
        name="back",
    )(centre, table, nears, cots, cotangent.reshape(square), msg_weight, self_weight)
    return (grad.reshape(features.shape), potential, energy[0, 0])


def solution(mesh):
    split = P("gx", "gy", "gz", None, None)
    in_specs = (split, P(), P(), P(), split, split)
    out_specs = (split, P("gx", "gy", "gz", None), P())
    return jax.shard_map(body, mesh=mesh, in_specs=in_specs, out_specs=out_specs, check_vma=False)
```

```python
import functools
import math

import jax
import jax.numpy as jnp
from jax import lax
from jax.experimental import pallas as pl
from jax.experimental.pallas import tpu as pltpu
from jax.sharding import PartitionSpec as P

PC = 16
LANES = 128
pair_scale = 0.1
coupling = 0.125
spread_width = 0.0625
highest = lax.Precision.HIGHEST
AXES = ("gx", "gy", "gz")
f32 = jnp.float32
bf16 = jnp.bfloat16
NT = (((1,), (1,)), ((), ()))
TN = (((0,), (0,)), ((), ()))


def full_spec(shape):
    return pl.BlockSpec(shape, lambda *_: (0,) * len(shape))


def cell_spec(shape):
    return pl.BlockSpec((1,) + tuple(shape[1:]), lambda i: (i,) + (0,) * (len(shape) - 1))


def split3(value):
    hi = lax.reduce_precision(value, 8, 7)
    rest = value - hi
    mid = lax.reduce_precision(rest, 8, 7)
    return hi, mid, rest - mid


def cas(first, second, length):
    angle = 2.0 * math.pi / length * (first[:, None] * second[None, :] % length).astype(f32)
    return jnp.cos(angle) + jnp.sin(angle)


def offsets():
    return [(i, j, k) for i in (-1, 0, 1) for j in (-1, 0, 1) for k in (-1, 0, 1)]


def offset_table():
    rows = []
    for o in offsets():
        norm = float(o[0] ** 2 + o[1] ** 2 + o[2] ** 2)
        doubled = [2.0 * v for v in o]
        rows.append([1.0] * 6 + doubled + [1.0] * 3 + [-v for v in doubled] + [-norm])
    return jnp.broadcast_to(jnp.array(rows, f32)[:, :, None], (27, 16, LANES)).astype(bf16)


def slot(offset, devices, length):
    if devices == 2 and length == 1:
        return 0 if offset == 0 else 1
    return 1 + offset


def coordinates(index, counts):
    return (index // (counts[1] * counts[2]), index // counts[2] % counts[1], index % counts[2])


def halo_plan(counts, lengths):
    doubled = [n == 2 and length == 1 for n, length in zip(counts, lengths)]
    own = [(0, 1) if two else (1, 1 + length) for two, length in zip(doubled, lengths)]

    def faces(d):
        if doubled[d]:
            return {1: ((0, 1), (1, 2))}
        length = lengths[d]
        return {1: ((length, length + 1), (0, 1)), -1: ((1, 2), (length + 1, length + 2))}

    moves = []

    def add(d, way, source, target, need):
        moves.append((d, way, tuple(source), tuple(target), need))
        return len(moves) - 1

    lines = [(own[1], None)]
    for way, (source, target) in faces(1).items():
        lines.append(
            (target, add(1, way, (own[0], source, own[2]), (own[0], target, own[2]), None))
        )
    sheets = []
    for at_y, need_y in lines:
        sheets.append((own[0], at_y, need_y))
        for way, (source, target) in faces(0).items():
            need = add(0, way, (source, at_y, own[2]), (target, at_y, own[2]), need_y)
            sheets.append((target, at_y, need))
    for at_x, at_y, need in sheets:
        for way, (source, target) in faces(2).items():
            add(2, way, (at_x, at_y, source), (at_x, at_y, target), need)
    padded = tuple(length + (1 if two else 2) for two, length in zip(doubled, lengths))
    return padded, own, moves


def halo_kernel(counts, lengths, src_ref, out_ref, send_sem, recv_sem, own_sem):
    padded, own, moves = halo_plan(counts, lengths)
    me = [lax.axis_index(a) for a in AXES]

    def neighbour(d, way):
        where = list(me)
        where[d] = lax.rem(me[d] + way + counts[d], counts[d])
        return tuple(where)

    barrier = pltpu.get_barrier_semaphore()
    links = sorted({(d, way) for d, way, *_ in moves})
    for d, way in links:
        pl.semaphore_signal(
            barrier, inc=1, device_id=neighbour(d, way), device_id_type=pl.DeviceIdType.MESH
        )
    pl.semaphore_wait(barrier, len(links))

    def region(ref, spans, shift=(0, 0, 0)):
        return ref.at[tuple(slice(lo - s, hi - s) for (lo, hi), s in zip(spans, shift))]

    starts = [lo for lo, _ in own]
    copies = []
    for which, (d, way, source, target, need) in enumerate(moves):
        origin = region(src_ref, source, starts) if need is None else region(out_ref, source)
        copies.append(
            pltpu.make_async_remote_copy(
                src_ref=origin,
                dst_ref=region(out_ref, target),
                send_sem=send_sem.at[which],
                recv_sem=recv_sem.at[which],
                device_id=neighbour(d, way),
                device_id_type=pl.DeviceIdType.MESH,
            )
        )
    keep = pltpu.make_async_copy(src_ref, region(out_ref, own), own_sem)
    ready = [w for w, m in enumerate(moves) if m[4] is None]
    for which in ready:
        copies[which].start()
    keep.start()
    waited = set()

    def forward(which):
        copies[which].wait_recv()
        waited.add(which)
        for later, move in enumerate(moves):
            if move[4] == which:
                copies[later].start()

    direct = [w for w in ready if moves[w][0] == 0]
    for which in direct:
        forward(which)
    for which in [w for w in ready if moves[w][0] == 1]:
        forward(which)
    for which, move in enumerate(moves):
        if which not in waited and any(m[4] == which for m in moves):
            forward(which)
    for which in range(len(moves)):
        if which not in waited:
            copies[which].wait_recv()
    for copy in copies:
        copy.wait_send()
    keep.wait()


def exchange_halo(shard, number, counts):
    lengths = shard.shape[:3]
    padded, _, moves = halo_plan(counts, lengths)
    return pl.pallas_call(
        functools.partial(halo_kernel, counts, lengths),
        out_shape=jax.ShapeDtypeStruct(padded + shard.shape[3:], shard.dtype),
        in_specs=[pl.BlockSpec(memory_space=pltpu.VMEM)],
        out_specs=pl.BlockSpec(memory_space=pl.ANY),
        scratch_shapes=[
            pltpu.SemaphoreType.DMA((len(moves),)),
            pltpu.SemaphoreType.DMA((len(moves),)),
            pltpu.SemaphoreType.DMA,
        ],
        compiler_params=params(collective_id=number, has_side_effects=True),
        name="halo",
    )(shard)


def swap_kernel(counts, senders, receivers, src_ref, out_ref, send_sem, recv_sem, own_sem):
    total = counts[0] * counts[1] * counts[2]
    chunks = src_ref.shape[0]
    me = (lax.axis_index("gx") * counts[1] + lax.axis_index("gy")) * counts[2] + lax.axis_index("gz")
    barrier = pltpu.get_barrier_semaphore()

    def chunk(q):
        return lax.rem(q, chunks)

    def greet(k, carry):
        pl.semaphore_signal(
            barrier,
            inc=1,
            device_id=coordinates(lax.rem(me + k, total), counts),
            device_id_type=pl.DeviceIdType.MESH,
        )
        return carry

    lax.fori_loop(1, total, greet, 0)
    keep = pltpu.make_async_copy(src_ref.at[chunk(me)], out_ref.at[me], own_sem)
    keep.start()
    pl.semaphore_wait(barrier, total - 1)

    def copy(k):
        to = lax.rem(me + k, total)
        return to, pltpu.make_async_remote_copy(
            src_ref=src_ref.at[chunk(to)],
            dst_ref=out_ref.at[me],
            send_sem=send_sem.at[k],
            recv_sem=recv_sem.at[k],
            device_id=coordinates(to, counts),
            device_id_type=pl.DeviceIdType.MESH,
        )

    def guarded(fact, act):
        if fact is None:
            act()
        else:
            pl.when(fact)(act)

    def sends(to):
        if senders < total:
            return me < senders
        return None if receivers == total else to < receivers

    def takes(source):
        if receivers < total:
            return me < receivers
        return None if senders == total else source < senders

    def begin(k, carry):
        to, move = copy(k)
        guarded(sends(to), lambda: move.start())
        return carry

    def finish(k, carry):
        to, move = copy(k)
        guarded(takes(lax.rem(me - k + total, total)), lambda: move.wait_recv())
        guarded(sends(to), lambda: move.wait_send())
        return carry

    lax.fori_loop(1, total, begin, 0)
    lax.fori_loop(1, total, finish, 0)
    keep.wait()


def exchange_planes(payload, number, counts, senders, receivers):
    total = counts[0] * counts[1] * counts[2]
    return pl.pallas_call(
        functools.partial(swap_kernel, counts, senders, receivers),
        out_shape=jax.ShapeDtypeStruct((total,) + payload.shape[1:], payload.dtype),
        in_specs=[pl.BlockSpec(memory_space=pltpu.VMEM)],
        out_specs=pl.BlockSpec(memory_space=pl.ANY),
        scratch_shapes=[
            pltpu.SemaphoreType.DMA((total,)),
            pltpu.SemaphoreType.DMA((total,)),
            pltpu.SemaphoreType.DMA,
        ],
        compiler_params=params(collective_id=number, has_side_effects=True),
        name="swap",
    )(payload)


def pair_total(cells, counts, centre, table_ref, near_ref, value_ref):
    index = pl.program_id(0)
    at_z = index % cells[2]
    at_y = index // cells[2] % cells[1]
    at_x = index // (cells[2] * cells[1])
    total = jnp.zeros((centre.shape[1], value_ref.shape[-1]), f32)
    for which, o in enumerate(offsets()):
        where = [
            base + slot(step, count, length)
            for base, step, count, length in zip((at_x, at_y, at_z), o, counts, cells)
        ]
        near = near_ref[where[0], where[1], where[2]] * table_ref[which]
        inside = lax.dot_general(centre, near, TN, preferred_element_type=f32)
        inside = jnp.maximum(inside, 0.0)
        weight = (pair_scale * inside * inside).astype(bf16)
        total = total + jnp.dot(
            weight, value_ref[where[0], where[1], where[2]], preferred_element_type=f32
        )
    return total


def message_kernel(
    cells, counts, centre_ref, table_ref, near_ref, value_ref, feature_ref, self_ref, read_ref, pre_ref, charge_ref
):
    message = pair_total(cells, counts, centre_ref[0], table_ref, near_ref, value_ref)
    preact = jnp.dot(feature_ref[0], self_ref[...], preferred_element_type=f32) + message
    pre_ref[0] = preact
    active = preact / (1.0 + jnp.exp(-preact))
    charge_ref[0] = lax.dot_general(
        read_ref[...], active, NT, precision=highest, preferred_element_type=f32
    )


def back_kernel(
    cells, counts, centre_ref, table_ref, near_ref, value_ref, cot_ref, msg_ref, self_ref, out_ref
):
    total = pair_total(cells, counts, centre_ref[0], table_ref, near_ref, value_ref)
    grad = lax.dot_general(total.astype(bf16), msg_ref[...], NT, preferred_element_type=f32)
    out_ref[0] = grad + lax.dot_general(
        cot_ref[0], self_ref[...], NT, preferred_element_type=f32
    )


def spline(corner, fraction, points, start=0):
    atoms = corner.shape[-1]
    offset = lax.broadcasted_iota(jnp.int32, (points, atoms), 0) - start - corner
    u = fraction
    first = (1.0 - u) * (1.0 - u) * (1.0 - u) / 6.0
    second = (3.0 * u * u * u - 6.0 * u * u + 4.0) / 6.0
    third = (-3.0 * u * u * u + 3.0 * u * u + 3.0 * u + 1.0) / 6.0
    fourth = u * u * u / 6.0
    zero = jnp.zeros((points, atoms), f32)
    return jnp.where(
        offset == 0,
        first,
        jnp.where(offset == 1, second, jnp.where(offset == 2, third, jnp.where(offset == 3, fourth, zero))),
    )


def spread_kernel(dims, corner_ref, fraction_ref, charge_ref, wave_ref, out_ref, hx_ref, left_ref):
    local_x, local_y, local_z, pack = dims
    rows_x = spline(corner_ref[0:1, :], fraction_ref[0:1, :], local_x)
    rows_y = spline(corner_ref[1:2, :], fraction_ref[1:2, :], local_y)
    hx_ref[...] = charge_ref[...] * jnp.dot(
        wave_ref[...], rows_x, precision=highest, preferred_element_type=f32
    )
    half = hx_ref.shape[0] // pack
    total = None
    for h in range(pack):

        def fill(k, carry):
            left_ref[pl.ds(pl.multiple_of(k * local_y, local_y), local_y), :] = (
                hx_ref[pl.ds(h * half + k, 1), :] * rows_y
            ).astype(bf16)
            return carry

        lax.fori_loop(0, half, fill, 0, unroll=8)
        right = spline(corner_ref[2:3, :], fraction_ref[2:3, :], LANES, h * local_z).astype(bf16)
        part = lax.dot_general(left_ref[...], right, NT, preferred_element_type=f32)
        total = part if total is None else total + part
    out_ref[...] = total.astype(bf16)


def plane_kernel(dims, count_x, got_ref, z_ref, y_ref, g_ref, out_ref):
    count_y, count_z, pack = dims
    rows = got_ref.shape[1]
    each = count_y * count_z
    halves = [None] * pack
    for c in range(count_z):
        stack = []
        for b in range(count_y):
            block = got_ref[b * count_z + c].astype(f32)
            for a in range(1, count_x):
                block = block + got_ref[a * each + b * count_z + c].astype(f32)
            stack.append(block)
        stack = jnp.concatenate(stack, axis=0)
        for h in range(pack):
            part = jnp.dot(stack, z_ref[c, h], precision=highest, preferred_element_type=f32)
            halves[h] = part if halves[h] is None else halves[h] + part
    lines = jnp.concatenate(halves, axis=0)
    wave = jnp.dot(y_ref[...], lines, precision=highest, preferred_element_type=f32)
    scaled = g_ref[...] * wave
    energy = jnp.sum(jnp.sum(scaled * wave, axis=1, keepdims=True), axis=0, keepdims=True)
    hi = energy.astype(bf16).astype(f32)
    mid = (energy - hi).astype(bf16).astype(f32)
    low = energy - hi - mid
    which = lax.broadcasted_iota(jnp.int32, (16, LANES), 0)
    tail = jnp.where(which == 0, hi, jnp.where(which == 1, mid, jnp.where(which == 2, low, 0.0)))
    back = lax.dot_general(y_ref[...], scaled, TN, precision=highest, preferred_element_type=f32)
    high = back.shape[0] // pack
    for c in range(count_z):
        total = None
        for h in range(pack):
            part = lax.dot_general(
                back[h * high : (h + 1) * high], z_ref[c, h], NT, precision=highest, preferred_element_type=f32
            )
            total = part if total is None else total + part
        for b in range(count_y):
            out_ref[b * count_z + c, 0:rows, :] = total[b * rows : (b + 1) * rows].astype(bf16)
            out_ref[b * count_z + c, rows : rows + 16, :] = tail.astype(bf16)


def field_kernel(dims, scale, escale, owners, corner_ref, fraction_ref, wave_ref, got_ref, out_ref, energy_ref, hx_ref):
    local_x, local_y, local_z, pack, rows = dims
    atoms = corner_ref.shape[-1]
    rows_x = spline(corner_ref[0:1, :], fraction_ref[0:1, :], local_x)
    rows_y = spline(corner_ref[1:2, :], fraction_ref[1:2, :], local_y)
    hx_ref[...] = jnp.dot(wave_ref[...], rows_x, precision=highest, preferred_element_type=f32)
    half = hx_ref.shape[0] // pack
    per = rows // local_y
    acc = jnp.zeros((local_y, atoms), f32)
    for h in range(pack):
        right = spline(corner_ref[2:3, :], fraction_ref[2:3, :], LANES, h * local_z).astype(bf16)

        def step(q, acc):
            block = got_ref[q, 0:rows, :]
            value = jnp.dot(block, right, preferred_element_type=f32)
            for k in range(per):
                acc = acc + value[k * local_y : (k + 1) * local_y] * hx_ref[
                    pl.ds(h * half + q * per + k, 1), :
                ]
            return acc

        acc = lax.fori_loop(0, owners, step, acc, unroll=4)
    value = scale * jnp.sum(acc * rows_y, axis=0, keepdims=True)
    out_ref[...] = jnp.broadcast_to(value, out_ref.shape)
    tail = jnp.zeros((16, LANES), f32)
    for q in range(owners):
        tail = tail + got_ref[q, rows : rows + 16, :].astype(f32)
    energy_ref[...] = jnp.broadcast_to(escale * jnp.sum(tail, axis=0, keepdims=True), energy_ref.shape)


def influence_of(index_x, index_y, index_z, size_x, size_y, size_z, points):
    def wave(index, size):
        signed = jnp.where(2 * index >= size, index - size, index)
        return signed.astype(f32) * (points / size)

    wave_x = wave(index_x, size_x)
    wave_y = wave(index_y, size_y)
    wave_z = wave(index_z, size_z)
    squared = wave_x * wave_x + wave_y * wave_y + wave_z * wave_z
    safe = jnp.where(squared > 0, squared, 1.0)
    return jnp.where(squared > 0, jnp.exp(-((math.pi * spread_width) ** 2) * squared) / safe, 0.0)


def params(**kw):
    return pltpu.CompilerParams(vmem_limit_bytes=48 * 1024 * 1024, **kw)


def body(features, msg_weight, self_weight, charge_weight, spline_corner, spline_fraction):
    cells = features.shape[:3]
    slots, width = features.shape[3:]
    number = cells[0] * cells[1] * cells[2]
    counts = tuple(lax.axis_size(a) for a in AXES)
    devices = counts[0] * counts[1] * counts[2]
    local = tuple(c * PC for c in cells)
    size = tuple(c * n for c, n in zip(local, counts))
    pack = LANES // local[2]
    planes = max(pack, size[0] // devices)
    owners = size[0] // planes
    inner = planes // pack
    rows = inner * local[1]
    atoms = number * slots
    volume = size[0] // PC * (size[1] // PC) * (size[2] // PC)

    flat = features.reshape(number * slots, width)
    projected = jnp.dot(flat, msg_weight, preferred_element_type=f32).astype(bf16).reshape(features.shape)
    position = lax.reduce_precision(
        (spline_corner.astype(f32) + 1.0 + spline_fraction) / PC, 8, 7
    )
    norm = jnp.sum(position * position, axis=3, keepdims=True)
    one = jnp.ones_like(norm)
    near = jnp.concatenate(
        [position, one, one, one, one, one, one, *split3(-norm), position, one], axis=3
    ).astype(bf16)
    centre = jnp.concatenate(
        [2.0 * position, *split3(1.0 - norm), position] + [one] * 7, axis=3
    ).astype(bf16).reshape(number, 16, slots)
    table = offset_table()

    padded = exchange_halo(jnp.concatenate([projected, near], axis=3), 0, counts)
    values = padded[:, :, :, :slots]
    nears = padded[:, :, :, slots:]

    read = jnp.broadcast_to(charge_weight.astype(f32)[None, :], (8, width))
    cell_features = features.reshape(number, slots, width)
    square = (number, slots, width)
    preact, charge = pl.pallas_call(
        functools.partial(message_kernel, cells, counts),
        out_shape=(jax.ShapeDtypeStruct(square, f32), jax.ShapeDtypeStruct((number, 8, slots), f32)),
        grid=(number,),
        in_specs=[
            cell_spec(centre.shape),
            full_spec(table.shape),
            full_spec(nears.shape),
            full_spec(values.shape),
            cell_spec(square),
            full_spec(self_weight.shape),
            full_spec(read.shape),
        ],
        out_specs=(cell_spec(square), cell_spec((number, 8, slots))),
        compiler_params=params(),
        name="message",
    )(centre, table, nears, values, cell_features, self_weight, read)

    shift = jnp.stack(
        [lax.broadcasted_iota(jnp.int32, cells + (slots,), d) * PC for d in range(3)], axis=0
    )
    corner = (spline_corner.transpose(3, 0, 1, 2, 4) + shift).reshape(3, atoms)
    fraction = spline_fraction.transpose(3, 0, 1, 2, 4).reshape(3, atoms)
    order = (
        jnp.arange(pack, dtype=jnp.int32)[:, None, None] * inner
        + jnp.arange(owners, dtype=jnp.int32)[None, :, None] * planes
        + jnp.arange(inner, dtype=jnp.int32)[None, None, :]
    ).reshape(-1)
    here = lax.axis_index("gx") * local[0] + jnp.arange(local[0], dtype=jnp.int32)
    wave_x = cas(order, here, size[0])
    charges = charge[:, 0, :].reshape(1, atoms)
    payload = pl.pallas_call(
        functools.partial(spread_kernel, (local[0], local[1], local[2], pack)),
        out_shape=jax.ShapeDtypeStruct((owners * rows, LANES), bf16),
        scratch_shapes=[
            pltpu.VMEM((size[0], atoms), f32),
            pltpu.VMEM((owners * rows, atoms), bf16),
        ],
        compiler_params=params(),
        name="spread",
    )(corner, fraction, charges, wave_x).reshape(owners, rows, LANES)
    got = exchange_planes(payload, 2, counts, devices, owners)

    range_y = jnp.arange(size[1], dtype=jnp.int32)
    range_z = jnp.arange(size[2], dtype=jnp.int32)
    cas_z = cas(range_z, range_z, size[2]).reshape(counts[2], 1, local[2], size[2])
    blank = jnp.zeros_like(cas_z)
    wide_z = jnp.concatenate(
        [
            jnp.concatenate([cas_z if at == h else blank for at in range(pack)], axis=2)
            for h in range(pack)
        ],
        axis=1,
    )
    cas_y = cas(range_y, range_y, size[1]).reshape(size[1], counts[1], local[1])
    same = jnp.eye(planes, dtype=f32).reshape(pack, inner, pack, inner)
    wide_y = jnp.einsum("abcd,kgy->abkcgdy", same, cas_y, precision=highest).reshape(
        planes * size[1], planes * size[1]
    )
    me = lax.axis_index(AXES)
    index_x = me * planes + jnp.arange(planes, dtype=jnp.int32)
    influence = influence_of(
        index_x[:, None, None], range_y[None, :, None], range_z[None, None, :], *size, PC
    ).reshape(planes * size[1], size[2])
    each = counts[1] * counts[2]
    solved = pl.pallas_call(
        functools.partial(plane_kernel, (counts[1], counts[2], pack), counts[0]),
        out_shape=jax.ShapeDtypeStruct((each, rows + 16, LANES), bf16),
        compiler_params=params(),
        name="planes",
    )(got, wide_z, wide_y, influence)
    field = exchange_planes(solved, 3, counts, owners, devices)

    potential, energy = pl.pallas_call(
        functools.partial(
            field_kernel,
            (local[0], local[1], local[2], pack, rows),
            coupling / volume,
            coupling / (2.0 * volume * atoms * devices),
            owners,
        ),
        out_shape=(jax.ShapeDtypeStruct((8, atoms), f32), jax.ShapeDtypeStruct((8, LANES), f32)),
        scratch_shapes=[pltpu.VMEM((size[0], atoms), f32)],
        compiler_params=params(),
        name="field",
    )(corner, fraction, wave_x, field)
    potential = potential[0].reshape(cells + (slots,))

    pre = preact.reshape(features.shape)
    sigma = jax.nn.sigmoid(pre)
    slope = sigma * (1.0 + pre * (1.0 - sigma))
    cotangent = (potential[..., None] * charge_weight.astype(f32) * slope).astype(bf16)
    cots = exchange_halo(cotangent, 1, counts)
    grad = pl.pallas_call(
        functools.partial(back_kernel, cells, counts),
        out_shape=jax.ShapeDtypeStruct(square, f32),
        grid=(number,),
        in_specs=[
            cell_spec(centre.shape),
            full_spec(table.shape),
            full_spec(nears.shape),
            full_spec(cots.shape),
            cell_spec(square),
            full_spec(msg_weight.shape),
            full_spec(self_weight.shape),
        ],
        out_specs=cell_spec(square),
        compiler_params=params(),
        name="back",
    )(centre, table, nears, cots, cotangent.reshape(square), msg_weight, self_weight)
    return (grad.reshape(features.shape), potential, energy[0, 0])


def solution(mesh):
    split = P("gx", "gy", "gz", None, None)
    in_specs = (split, P(), P(), P(), split, split)
    out_specs = (split, P("gx", "gy", "gz", None), P())
    return jax.shard_map(body, mesh=mesh, in_specs=in_specs, out_specs=out_specs, check_vma=False)
```

```python
import functools
import math

import jax
import jax.numpy as jnp
from jax import lax
from jax.experimental import pallas as pl
from jax.experimental.pallas import tpu as pltpu
from jax.sharding import PartitionSpec as P

PC = 16
LANES = 128
pair_scale = 0.1
coupling = 0.125
spread_width = 0.0625
highest = lax.Precision.HIGHEST
AXES = ("gx", "gy", "gz")
f32 = jnp.float32
bf16 = jnp.bfloat16
NT = (((1,), (1,)), ((), ()))
TN = (((0,), (0,)), ((), ()))


def full_spec(shape):
    return pl.BlockSpec(shape, lambda *_: (0,) * len(shape))


def cell_spec(shape):
    return pl.BlockSpec((1,) + tuple(shape[1:]), lambda i: (i,) + (0,) * (len(shape) - 1))


def split3(value):
    hi = lax.reduce_precision(value, 8, 7)
    rest = value - hi
    mid = lax.reduce_precision(rest, 8, 7)
    return hi, mid, rest - mid


def cas(first, second, length):
    angle = 2.0 * math.pi / length * (first[:, None] * second[None, :] % length).astype(f32)
    return jnp.cos(angle) + jnp.sin(angle)


def offsets():
    return [(i, j, k) for i in (-1, 0, 1) for j in (-1, 0, 1) for k in (-1, 0, 1)]


def offset_table():
    rows = []
    for o in offsets():
        norm = float(o[0] ** 2 + o[1] ** 2 + o[2] ** 2)
        doubled = [2.0 * v for v in o]
        rows.append([1.0] * 6 + doubled + [1.0] * 3 + [-v for v in doubled] + [-norm])
    return jnp.broadcast_to(jnp.array(rows, f32)[:, :, None], (27, 16, LANES)).astype(bf16)


def slot(offset, devices, length):
    if devices == 2 and length == 1:
        return 0 if offset == 0 else 1
    return 1 + offset


def coordinates(index, counts):
    return (index // (counts[1] * counts[2]), index // counts[2] % counts[1], index % counts[2])


def halo_plan(counts, lengths):
    doubled = [n == 2 and length == 1 for n, length in zip(counts, lengths)]
    own = [(0, 1) if two else (1, 1 + length) for two, length in zip(doubled, lengths)]

    def faces(d):
        if doubled[d]:
            return {1: ((0, 1), (1, 2))}
        length = lengths[d]
        return {1: ((length, length + 1), (0, 1)), -1: ((1, 2), (length + 1, length + 2))}

    moves = []

    def add(d, way, source, target, need):
        moves.append((d, way, tuple(source), tuple(target), need))
        return len(moves) - 1

    lines = [(own[2], None)]
    for way, (source, target) in faces(2).items():
        lines.append(
            (target, add(2, way, (own[0], own[1], source), (own[0], own[1], target), None))
        )
    sheets = []
    for at_z, need_z in lines:
        sheets.append((own[1], at_z, need_z))
        for way, (source, target) in faces(1).items():
            need = add(1, way, (own[0], source, at_z), (own[0], target, at_z), need_z)
            sheets.append((target, at_z, need))
    for at_y, at_z, need in sheets:
        for way, (source, target) in faces(0).items():
            add(0, way, (source, at_y, at_z), (target, at_y, at_z), need)
    padded = tuple(length + (1 if two else 2) for two, length in zip(doubled, lengths))
    return padded, own, moves


def halo_kernel(counts, lengths, src_ref, out_ref, send_sem, recv_sem, own_sem):
    padded, own, moves = halo_plan(counts, lengths)
    me = [lax.axis_index(a) for a in AXES]

    def neighbour(d, way):
        where = list(me)
        where[d] = lax.rem(me[d] + way + counts[d], counts[d])
        return tuple(where)

    barrier = pltpu.get_barrier_semaphore()
    links = sorted({(d, way) for d, way, *_ in moves})
    for d, way in links:
        pl.semaphore_signal(
            barrier, inc=1, device_id=neighbour(d, way), device_id_type=pl.DeviceIdType.MESH
        )
    pl.semaphore_wait(barrier, len(links))

    def region(ref, spans, shift=(0, 0, 0)):
        return ref.at[tuple(slice(lo - s, hi - s) for (lo, hi), s in zip(spans, shift))]

    starts = [lo for lo, _ in own]
    copies = []
    for which, (d, way, source, target, need) in enumerate(moves):
        origin = region(src_ref, source, starts) if need is None else region(out_ref, source)
        copies.append(
            pltpu.make_async_remote_copy(
                src_ref=origin,
                dst_ref=region(out_ref, target),
                send_sem=send_sem.at[which],
                recv_sem=recv_sem.at[which],
                device_id=neighbour(d, way),
                device_id_type=pl.DeviceIdType.MESH,
            )
        )
    keep = pltpu.make_async_copy(src_ref, region(out_ref, own), own_sem)
    ready = [w for w, m in enumerate(moves) if m[4] is None]
    for which in ready:
        copies[which].start()
    keep.start()
    waited = set()

    def forward(which):
        copies[which].wait_recv()
        waited.add(which)
        for later, move in enumerate(moves):
            if move[4] == which:
                copies[later].start()

    for which, move in enumerate(moves):
        if which not in waited and any(m[4] == which for m in moves):
            forward(which)
    for which in range(len(moves)):
        if which not in waited:
            copies[which].wait_recv()
    for copy in copies:
        copy.wait_send()
    keep.wait()


def exchange_halo(shard, number, counts):
    lengths = shard.shape[:3]
    padded, _, moves = halo_plan(counts, lengths)
    return pl.pallas_call(
        functools.partial(halo_kernel, counts, lengths),
        out_shape=jax.ShapeDtypeStruct(padded + shard.shape[3:], shard.dtype),
        in_specs=[pl.BlockSpec(memory_space=pltpu.VMEM)],
        out_specs=pl.BlockSpec(memory_space=pl.ANY),
        scratch_shapes=[
            pltpu.SemaphoreType.DMA((len(moves),)),
            pltpu.SemaphoreType.DMA((len(moves),)),
            pltpu.SemaphoreType.DMA,
        ],
        compiler_params=params(collective_id=number, has_side_effects=True),
        name="halo",
    )(shard)


def swap_kernel(counts, senders, receivers, src_ref, out_ref, send_sem, recv_sem, own_sem):
    total = counts[0] * counts[1] * counts[2]
    chunks = src_ref.shape[0]
    me = (lax.axis_index("gx") * counts[1] + lax.axis_index("gy")) * counts[2] + lax.axis_index("gz")
    barrier = pltpu.get_barrier_semaphore()

    def chunk(q):
        return lax.rem(q, chunks)

    def greet(k, carry):
        pl.semaphore_signal(
            barrier,
            inc=1,
            device_id=coordinates(lax.rem(me + k, total), counts),
            device_id_type=pl.DeviceIdType.MESH,
        )
        return carry

    lax.fori_loop(1, total, greet, 0)
    keep = pltpu.make_async_copy(src_ref.at[chunk(me)], out_ref.at[me], own_sem)
    keep.start()
    pl.semaphore_wait(barrier, total - 1)

    def copy(k):
        to = lax.rem(me + k, total)
        return to, pltpu.make_async_remote_copy(
            src_ref=src_ref.at[chunk(to)],
            dst_ref=out_ref.at[me],
            send_sem=send_sem.at[k],
            recv_sem=recv_sem.at[k],
            device_id=coordinates(to, counts),
            device_id_type=pl.DeviceIdType.MESH,
        )

    def guarded(fact, act):
        if fact is None:
            act()
        else:
            pl.when(fact)(act)

    def sends(to):
        if senders < total:
            return me < senders
        return None if receivers == total else to < receivers

    def takes(source):
        if receivers < total:
            return me < receivers
        return None if senders == total else source < senders

    def begin(k, carry):
        to, move = copy(k)
        guarded(sends(to), lambda: move.start())
        return carry

    def finish(k, carry):
        to, move = copy(k)
        guarded(takes(lax.rem(me - k + total, total)), lambda: move.wait_recv())
        guarded(sends(to), lambda: move.wait_send())
        return carry

    lax.fori_loop(1, total, begin, 0)
    lax.fori_loop(1, total, finish, 0)
    keep.wait()


def exchange_planes(payload, number, counts, senders, receivers):
    total = counts[0] * counts[1] * counts[2]
    return pl.pallas_call(
        functools.partial(swap_kernel, counts, senders, receivers),
        out_shape=jax.ShapeDtypeStruct((total,) + payload.shape[1:], payload.dtype),
        in_specs=[pl.BlockSpec(memory_space=pltpu.VMEM)],
        out_specs=pl.BlockSpec(memory_space=pl.ANY),
        scratch_shapes=[
            pltpu.SemaphoreType.DMA((total,)),
            pltpu.SemaphoreType.DMA((total,)),
            pltpu.SemaphoreType.DMA,
        ],
        compiler_params=params(collective_id=number, has_side_effects=True),
        name="swap",
    )(payload)


def pair_total(cells, counts, centre, table_ref, near_ref, value_ref):
    index = pl.program_id(0)
    at_z = index % cells[2]
    at_y = index // cells[2] % cells[1]
    at_x = index // (cells[2] * cells[1])
    total = None

    def cell_at(o):
        return tuple(
            base + slot(step, count, length)
            for base, step, count, length in zip((at_x, at_y, at_z), o, counts, cells)
        )

    every = list(enumerate(offsets()))
    for first in range(0, len(every), 2):
        group = every[first : first + 2]
        near = jnp.concatenate([near_ref[cell_at(o)] * table_ref[w] for w, o in group], axis=1)
        values = jnp.concatenate([value_ref[cell_at(o)] for _, o in group], axis=0)
        inside = lax.dot_general(centre, near, TN, preferred_element_type=f32)
        inside = jnp.maximum(inside, 0.0)
        weight = (pair_scale * inside * inside).astype(bf16)
        part = jnp.dot(weight, values, preferred_element_type=f32)
        total = part if total is None else total + part
    return total


def message_kernel(
    cells, counts, centre_ref, table_ref, near_ref, value_ref, feature_ref, self_ref, read_ref, pre_ref, charge_ref
):
    message = pair_total(cells, counts, centre_ref[0], table_ref, near_ref, value_ref)
    preact = jnp.dot(feature_ref[0], self_ref[...], preferred_element_type=f32) + message
    pre_ref[0] = preact
    active = preact / (1.0 + jnp.exp(-preact))
    charge_ref[0] = lax.dot_general(
        read_ref[...], active, NT, precision=highest, preferred_element_type=f32
    )


def back_kernel(
    cells, counts, centre_ref, table_ref, near_ref, value_ref, cot_ref, msg_ref, self_ref, out_ref
):
    total = pair_total(cells, counts, centre_ref[0], table_ref, near_ref, value_ref)
    grad = lax.dot_general(total.astype(bf16), msg_ref[...], NT, preferred_element_type=f32)
    out_ref[0] = grad + lax.dot_general(
        cot_ref[0], self_ref[...], NT, preferred_element_type=f32
    )


def spline(corner, fraction, points, start=0):
    atoms = corner.shape[-1]
    offset = lax.broadcasted_iota(jnp.int32, (points, atoms), 0) - start - corner
    u = fraction
    first = (1.0 - u) * (1.0 - u) * (1.0 - u) / 6.0
    second = (3.0 * u * u * u - 6.0 * u * u + 4.0) / 6.0
    third = (-3.0 * u * u * u + 3.0 * u * u + 3.0 * u + 1.0) / 6.0
    fourth = u * u * u / 6.0
    zero = jnp.zeros((points, atoms), f32)
    return jnp.where(
        offset == 0,
        first,
        jnp.where(offset == 1, second, jnp.where(offset == 2, third, jnp.where(offset == 3, fourth, zero))),
    )


def spread_kernel(dims, corner_ref, fraction_ref, charge_ref, wave_ref, out_ref, hx_ref, left_ref):
    local_x, local_y, local_z, pack = dims
    rows_x = spline(corner_ref[0:1, :], fraction_ref[0:1, :], local_x)
    rows_y = spline(corner_ref[1:2, :], fraction_ref[1:2, :], local_y)
    hx_ref[...] = charge_ref[...] * jnp.dot(
        wave_ref[...], rows_x, precision=highest, preferred_element_type=f32
    )
    half = hx_ref.shape[0] // pack
    total = None
    for h in range(pack):

        def fill(k, carry):
            left_ref[pl.ds(pl.multiple_of(k * local_y, local_y), local_y), :] = (
                hx_ref[pl.ds(h * half + k, 1), :] * rows_y
            ).astype(bf16)
            return carry

        lax.fori_loop(0, half, fill, 0, unroll=8)
        right = spline(corner_ref[2:3, :], fraction_ref[2:3, :], LANES, h * local_z).astype(bf16)
        part = lax.dot_general(left_ref[...], right, NT, preferred_element_type=f32)
        total = part if total is None else total + part
    out_ref[...] = total.astype(bf16)


def plane_kernel(dims, count_x, got_ref, z_ref, y_ref, g_ref, out_ref):
    count_y, count_z, pack = dims
    rows = got_ref.shape[1]
    each = count_y * count_z
    halves = [None] * pack
    for c in range(count_z):
        stack = []
        for b in range(count_y):
            block = got_ref[b * count_z + c].astype(f32)
            for a in range(1, count_x):
                block = block + got_ref[a * each + b * count_z + c].astype(f32)
            stack.append(block)
        stack = jnp.concatenate(stack, axis=0)
        for h in range(pack):
            part = jnp.dot(stack, z_ref[c, h], precision=highest, preferred_element_type=f32)
            halves[h] = part if halves[h] is None else halves[h] + part
    lines = jnp.concatenate(halves, axis=0)
    wave = jnp.dot(y_ref[...], lines, precision=highest, preferred_element_type=f32)
    scaled = g_ref[...] * wave
    energy = jnp.sum(jnp.sum(scaled * wave, axis=1, keepdims=True), axis=0, keepdims=True)
    hi = energy.astype(bf16).astype(f32)
    mid = (energy - hi).astype(bf16).astype(f32)
    low = energy - hi - mid
    which = lax.broadcasted_iota(jnp.int32, (16, LANES), 0)
    tail = jnp.where(which == 0, hi, jnp.where(which == 1, mid, jnp.where(which == 2, low, 0.0)))
    back = lax.dot_general(y_ref[...], scaled, TN, precision=highest, preferred_element_type=f32)
    high = back.shape[0] // pack
    for c in range(count_z):
        total = None
        for h in range(pack):
            part = lax.dot_general(
                back[h * high : (h + 1) * high], z_ref[c, h], NT, precision=highest, preferred_element_type=f32
            )
            total = part if total is None else total + part
        for b in range(count_y):
            out_ref[b * count_z + c, 0:rows, :] = total[b * rows : (b + 1) * rows].astype(bf16)
            out_ref[b * count_z + c, rows : rows + 16, :] = tail.astype(bf16)


def field_kernel(dims, scale, escale, owners, corner_ref, fraction_ref, wave_ref, got_ref, out_ref, energy_ref, hx_ref):
    local_x, local_y, local_z, pack, rows = dims
    atoms = corner_ref.shape[-1]
    rows_x = spline(corner_ref[0:1, :], fraction_ref[0:1, :], local_x)
    rows_y = spline(corner_ref[1:2, :], fraction_ref[1:2, :], local_y)
    hx_ref[...] = jnp.dot(wave_ref[...], rows_x, precision=highest, preferred_element_type=f32)
    half = hx_ref.shape[0] // pack
    per = rows // local_y
    acc = jnp.zeros((local_y, atoms), f32)
    for h in range(pack):
        right = spline(corner_ref[2:3, :], fraction_ref[2:3, :], LANES, h * local_z).astype(bf16)

        def step(q, acc):
            block = got_ref[q, 0:rows, :]
            value = jnp.dot(block, right, preferred_element_type=f32)
            for k in range(per):
                acc = acc + value[k * local_y : (k + 1) * local_y] * hx_ref[
                    pl.ds(h * half + q * per + k, 1), :
                ]
            return acc

        acc = lax.fori_loop(0, owners, step, acc, unroll=4)
    value = scale * jnp.sum(acc * rows_y, axis=0, keepdims=True)
    out_ref[...] = jnp.broadcast_to(value, out_ref.shape)
    tail = jnp.zeros((16, LANES), f32)
    for q in range(owners):
        tail = tail + got_ref[q, rows : rows + 16, :].astype(f32)
    energy_ref[...] = jnp.broadcast_to(escale * jnp.sum(tail, axis=0, keepdims=True), energy_ref.shape)


def influence_of(index_x, index_y, index_z, size_x, size_y, size_z, points):
    def wave(index, size):
        signed = jnp.where(2 * index >= size, index - size, index)
        return signed.astype(f32) * (points / size)

    wave_x = wave(index_x, size_x)
    wave_y = wave(index_y, size_y)
    wave_z = wave(index_z, size_z)
    squared = wave_x * wave_x + wave_y * wave_y + wave_z * wave_z
    safe = jnp.where(squared > 0, squared, 1.0)
    return jnp.where(squared > 0, jnp.exp(-((math.pi * spread_width) ** 2) * squared) / safe, 0.0)


def params(**kw):
    return pltpu.CompilerParams(vmem_limit_bytes=48 * 1024 * 1024, **kw)


def body(features, msg_weight, self_weight, charge_weight, spline_corner, spline_fraction):
    cells = features.shape[:3]
    slots, width = features.shape[3:]
    number = cells[0] * cells[1] * cells[2]
    counts = tuple(lax.axis_size(a) for a in AXES)
    devices = counts[0] * counts[1] * counts[2]
    local = tuple(c * PC for c in cells)
    size = tuple(c * n for c, n in zip(local, counts))
    pack = LANES // local[2]
    planes = max(pack, size[0] // devices)
    owners = size[0] // planes
    inner = planes // pack
    rows = inner * local[1]
    atoms = number * slots
    volume = size[0] // PC * (size[1] // PC) * (size[2] // PC)

    flat = features.reshape(number * slots, width)
    projected = jnp.dot(flat, msg_weight, preferred_element_type=f32).astype(bf16).reshape(features.shape)
    position = lax.reduce_precision(
        (spline_corner.astype(f32) + 1.0 + spline_fraction) / PC, 8, 7
    )
    norm = jnp.sum(position * position, axis=3, keepdims=True)
    one = jnp.ones_like(norm)
    near = jnp.concatenate(
        [position, one, one, one, one, one, one, *split3(-norm), position, one], axis=3
    ).astype(bf16)
    centre = jnp.concatenate(
        [2.0 * position, *split3(1.0 - norm), position] + [one] * 7, axis=3
    ).astype(bf16).reshape(number, 16, slots)
    table = offset_table()

    padded = exchange_halo(jnp.concatenate([projected, near], axis=3), 0, counts)
    values = padded[:, :, :, :slots]
    nears = padded[:, :, :, slots:]

    read = jnp.broadcast_to(charge_weight.astype(f32)[None, :], (8, width))
    cell_features = features.reshape(number, slots, width)
    square = (number, slots, width)
    preact, charge = pl.pallas_call(
        functools.partial(message_kernel, cells, counts),
        out_shape=(jax.ShapeDtypeStruct(square, f32), jax.ShapeDtypeStruct((number, 8, slots), f32)),
        grid=(number,),
        in_specs=[
            cell_spec(centre.shape),
            full_spec(table.shape),
            full_spec(nears.shape),
            full_spec(values.shape),
            cell_spec(square),
            full_spec(self_weight.shape),
            full_spec(read.shape),
        ],
        out_specs=(cell_spec(square), cell_spec((number, 8, slots))),
        compiler_params=params(),
        name="message",
    )(centre, table, nears, values, cell_features, self_weight, read)

    shift = jnp.stack(
        [lax.broadcasted_iota(jnp.int32, cells + (slots,), d) * PC for d in range(3)], axis=0
    )
    corner = (spline_corner.transpose(3, 0, 1, 2, 4) + shift).reshape(3, atoms)
    fraction = spline_fraction.transpose(3, 0, 1, 2, 4).reshape(3, atoms)
    order = (
        jnp.arange(pack, dtype=jnp.int32)[:, None, None] * inner
        + jnp.arange(owners, dtype=jnp.int32)[None, :, None] * planes
        + jnp.arange(inner, dtype=jnp.int32)[None, None, :]
    ).reshape(-1)
    here = lax.axis_index("gx") * local[0] + jnp.arange(local[0], dtype=jnp.int32)
    wave_x = cas(order, here, size[0])
    charges = charge[:, 0, :].reshape(1, atoms)
    payload = pl.pallas_call(
        functools.partial(spread_kernel, (local[0], local[1], local[2], pack)),
        out_shape=jax.ShapeDtypeStruct((owners * rows, LANES), bf16),
        scratch_shapes=[
            pltpu.VMEM((size[0], atoms), f32),
            pltpu.VMEM((owners * rows, atoms), bf16),
        ],
        compiler_params=params(),
        name="spread",
    )(corner, fraction, charges, wave_x).reshape(owners, rows, LANES)
    got = exchange_planes(payload, 2, counts, devices, owners)

    range_y = jnp.arange(size[1], dtype=jnp.int32)
    range_z = jnp.arange(size[2], dtype=jnp.int32)
    cas_z = cas(range_z, range_z, size[2]).reshape(counts[2], 1, local[2], size[2])
    blank = jnp.zeros_like(cas_z)
    wide_z = jnp.concatenate(
        [
            jnp.concatenate([cas_z if at == h else blank for at in range(pack)], axis=2)
            for h in range(pack)
        ],
        axis=1,
    )
    cas_y = cas(range_y, range_y, size[1]).reshape(size[1], counts[1], local[1])
    same = jnp.eye(planes, dtype=f32).reshape(pack, inner, pack, inner)
    wide_y = jnp.einsum("abcd,kgy->abkcgdy", same, cas_y, precision=highest).reshape(
        planes * size[1], planes * size[1]
    )
    me = lax.axis_index(AXES)
    index_x = me * planes + jnp.arange(planes, dtype=jnp.int32)
    influence = influence_of(
        index_x[:, None, None], range_y[None, :, None], range_z[None, None, :], *size, PC
    ).reshape(planes * size[1], size[2])
    each = counts[1] * counts[2]
    solved = pl.pallas_call(
        functools.partial(plane_kernel, (counts[1], counts[2], pack), counts[0]),
        out_shape=jax.ShapeDtypeStruct((each, rows + 16, LANES), bf16),
        compiler_params=params(),
        name="planes",
    )(got, wide_z, wide_y, influence)
    field = exchange_planes(solved, 3, counts, owners, devices)

    potential, energy = pl.pallas_call(
        functools.partial(
            field_kernel,
            (local[0], local[1], local[2], pack, rows),
            coupling / volume,
            coupling / (2.0 * volume * atoms * devices),
            owners,
        ),
        out_shape=(jax.ShapeDtypeStruct((8, atoms), f32), jax.ShapeDtypeStruct((8, LANES), f32)),
        scratch_shapes=[pltpu.VMEM((size[0], atoms), f32)],
        compiler_params=params(),
        name="field",
    )(corner, fraction, wave_x, field)
    potential = potential[0].reshape(cells + (slots,))

    pre = preact.reshape(features.shape)
    sigma = jax.nn.sigmoid(pre)
    slope = sigma * (1.0 + pre * (1.0 - sigma))
    cotangent = (potential[..., None] * charge_weight.astype(f32) * slope).astype(bf16)
    cots = exchange_halo(cotangent, 1, counts)
    grad = pl.pallas_call(
        functools.partial(back_kernel, cells, counts),
        out_shape=jax.ShapeDtypeStruct(square, f32),
        grid=(number,),
        in_specs=[
            cell_spec(centre.shape),
            full_spec(table.shape),
            full_spec(nears.shape),
            full_spec(cots.shape),
            cell_spec(square),
            full_spec(msg_weight.shape),
            full_spec(self_weight.shape),
        ],
        out_specs=cell_spec(square),
        compiler_params=params(),
        name="back",
    )(centre, table, nears, cots, cotangent.reshape(square), msg_weight, self_weight)
    return (grad.reshape(features.shape), potential, energy[0, 0])


def solution(mesh):
    split = P("gx", "gy", "gz", None, None)
    in_specs = (split, P(), P(), P(), split, split)
    out_specs = (split, P("gx", "gy", "gz", None), P())
    return jax.shard_map(body, mesh=mesh, in_specs=in_specs, out_specs=out_specs, check_vma=False)
```

```python
import functools
import math

import jax
import jax.numpy as jnp
from jax import lax
from jax.experimental import pallas as pl
from jax.experimental.pallas import tpu as pltpu
from jax.sharding import PartitionSpec as P

PC = 16
LANES = 128
pair_scale = 0.1
coupling = 0.125
spread_width = 0.0625
highest = lax.Precision.HIGHEST
AXES = ("gx", "gy", "gz")
f32 = jnp.float32
bf16 = jnp.bfloat16
NT = (((1,), (1,)), ((), ()))
TN = (((0,), (0,)), ((), ()))


def full_spec(shape):
    return pl.BlockSpec(shape, lambda *_: (0,) * len(shape))


def cell_spec(shape):
    return pl.BlockSpec((1,) + tuple(shape[1:]), lambda i: (i,) + (0,) * (len(shape) - 1))


def split3(value):
    hi = lax.reduce_precision(value, 8, 7)
    rest = value - hi
    mid = lax.reduce_precision(rest, 8, 7)
    return hi, mid, rest - mid


def cas(first, second, length):
    angle = 2.0 * math.pi / length * (first[:, None] * second[None, :] % length).astype(f32)
    return jnp.cos(angle) + jnp.sin(angle)


def offsets():
    return [(i, j, k) for i in (-1, 0, 1) for j in (-1, 0, 1) for k in (-1, 0, 1)]


def offset_table():
    rows = []
    for o in offsets():
        norm = float(o[0] ** 2 + o[1] ** 2 + o[2] ** 2)
        doubled = [2.0 * v for v in o]
        rows.append([1.0] * 6 + doubled + [1.0] * 3 + [-v for v in doubled] + [-norm])
    return jnp.broadcast_to(jnp.array(rows, f32)[:, :, None], (27, 16, LANES)).astype(bf16)


def slot(offset, devices, length):
    if devices == 2 and length == 1:
        return 0 if offset == 0 else 1
    return 1 + offset


def coordinates(index, counts):
    return (index // (counts[1] * counts[2]), index // counts[2] % counts[1], index % counts[2])


def halo_plan(counts, lengths):
    doubled = [n == 2 and length == 1 for n, length in zip(counts, lengths)]
    own = [(0, 1) if two else (1, 1 + length) for two, length in zip(doubled, lengths)]

    def faces(d):
        if doubled[d]:
            return {1: ((0, 1), (1, 2))}
        length = lengths[d]
        return {1: ((length, length + 1), (0, 1)), -1: ((1, 2), (length + 1, length + 2))}

    moves = []

    def add(d, way, source, target, need):
        moves.append((d, way, tuple(source), tuple(target), need))
        return len(moves) - 1

    lines = [(own[2], None)]
    for way, (source, target) in faces(2).items():
        lines.append(
            (target, add(2, way, (own[0], own[1], source), (own[0], own[1], target), None))
        )
    sheets = []
    for at_z, need_z in lines:
        sheets.append((own[1], at_z, need_z))
        for way, (source, target) in faces(1).items():
            need = add(1, way, (own[0], source, at_z), (own[0], target, at_z), need_z)
            sheets.append((target, at_z, need))
    for at_y, at_z, need in sheets:
        for way, (source, target) in faces(0).items():
            add(0, way, (source, at_y, at_z), (target, at_y, at_z), need)
    padded = tuple(length + (1 if two else 2) for two, length in zip(doubled, lengths))
    return padded, own, moves


def halo_kernel(counts, lengths, src_ref, out_ref, send_sem, recv_sem, own_sem):
    padded, own, moves = halo_plan(counts, lengths)
    me = [lax.axis_index(a) for a in AXES]

    def neighbour(d, way):
        where = list(me)
        where[d] = lax.rem(me[d] + way + counts[d], counts[d])
        return tuple(where)

    barrier = pltpu.get_barrier_semaphore()
    links = sorted({(d, way) for d, way, *_ in moves})
    for d, way in links:
        pl.semaphore_signal(
            barrier, inc=1, device_id=neighbour(d, way), device_id_type=pl.DeviceIdType.MESH
        )
    pl.semaphore_wait(barrier, len(links))

    def region(ref, spans, shift=(0, 0, 0)):
        return ref.at[tuple(slice(lo - s, hi - s) for (lo, hi), s in zip(spans, shift))]

    starts = [lo for lo, _ in own]
    copies = []
    for which, (d, way, source, target, need) in enumerate(moves):
        origin = region(src_ref, source, starts) if need is None else region(out_ref, source)
        copies.append(
            pltpu.make_async_remote_copy(
                src_ref=origin,
                dst_ref=region(out_ref, target),
                send_sem=send_sem.at[which],
                recv_sem=recv_sem.at[which],
                device_id=neighbour(d, way),
                device_id_type=pl.DeviceIdType.MESH,
            )
        )
    keep = pltpu.make_async_copy(src_ref, region(out_ref, own), own_sem)
    ready = [w for w, m in enumerate(moves) if m[4] is None]
    for which in ready:
        copies[which].start()
    keep.start()
    waited = set()

    def forward(which):
        copies[which].wait_recv()
        waited.add(which)
        for later, move in enumerate(moves):
            if move[4] == which:
                copies[later].start()

    for which, move in enumerate(moves):
        if which not in waited and any(m[4] == which for m in moves):
            forward(which)
    for which in range(len(moves)):
        if which not in waited:
            copies[which].wait_recv()
    for copy in copies:
        copy.wait_send()
    keep.wait()


def exchange_halo(shard, number, counts):
    lengths = shard.shape[:3]
    padded, _, moves = halo_plan(counts, lengths)
    return pl.pallas_call(
        functools.partial(halo_kernel, counts, lengths),
        out_shape=jax.ShapeDtypeStruct(padded + shard.shape[3:], shard.dtype),
        in_specs=[pl.BlockSpec(memory_space=pltpu.VMEM)],
        out_specs=pl.BlockSpec(memory_space=pl.ANY),
        scratch_shapes=[
            pltpu.SemaphoreType.DMA((len(moves),)),
            pltpu.SemaphoreType.DMA((len(moves),)),
            pltpu.SemaphoreType.DMA,
        ],
        compiler_params=params(collective_id=number, has_side_effects=True),
        name="halo",
    )(shard)


def pair_total(cells, counts, centre, table_ref, near_ref, value_ref):
    index = pl.program_id(0)
    at_z = index % cells[2]
    at_y = index // cells[2] % cells[1]
    at_x = index // (cells[2] * cells[1])
    total = None

    def cell_at(o):
        return tuple(
            base + slot(step, count, length)
            for base, step, count, length in zip((at_x, at_y, at_z), o, counts, cells)
        )

    for which, o in enumerate(offsets()):
        near = near_ref[cell_at(o)] * table_ref[which]
        inside = lax.dot_general(centre, near, TN, preferred_element_type=f32)
        inside = jnp.maximum(inside, 0.0)
        weight = (pair_scale * inside * inside).astype(bf16)
        part = jnp.dot(weight, value_ref[cell_at(o)], preferred_element_type=f32)
        total = part if total is None else total + part
    return total


def message_kernel(
    cells, counts, centre_ref, table_ref, near_ref, value_ref, feature_ref, self_ref, read_ref, pre_ref, charge_ref
):
    message = pair_total(cells, counts, centre_ref[0], table_ref, near_ref, value_ref)
    preact = jnp.dot(feature_ref[0], self_ref[...], preferred_element_type=f32) + message
    pre_ref[0] = preact
    active = preact / (1.0 + jnp.exp(-preact))
    charge_ref[0] = lax.dot_general(
        read_ref[...], active, NT, precision=highest, preferred_element_type=f32
    )


def back_kernel(
    cells, counts, centre_ref, table_ref, near_ref, value_ref, cot_ref, msg_ref, self_ref, out_ref
):
    total = pair_total(cells, counts, centre_ref[0], table_ref, near_ref, value_ref)
    grad = lax.dot_general(total.astype(bf16), msg_ref[...], NT, preferred_element_type=f32)
    out_ref[0] = grad + lax.dot_general(
        cot_ref[0], self_ref[...], NT, preferred_element_type=f32
    )


def spline(corner, fraction, points, start=0):
    atoms = corner.shape[-1]
    offset = lax.broadcasted_iota(jnp.int32, (points, atoms), 0) - start - corner
    u = fraction
    first = (1.0 - u) * (1.0 - u) * (1.0 - u) / 6.0
    second = (3.0 * u * u * u - 6.0 * u * u + 4.0) / 6.0
    third = (-3.0 * u * u * u + 3.0 * u * u + 3.0 * u + 1.0) / 6.0
    fourth = u * u * u / 6.0
    zero = jnp.zeros((points, atoms), f32)
    return jnp.where(
        offset == 0,
        first,
        jnp.where(offset == 1, second, jnp.where(offset == 2, third, jnp.where(offset == 3, fourth, zero))),
    )


def solve_planes(counts, pack, got_ref, z_ref, y_ref, g_ref, out_ref):
    count_x, count_y, count_z = counts
    rows = got_ref.shape[1]
    each = count_y * count_z
    halves = [None] * pack
    for c in range(count_z):
        stack = []
        for b in range(count_y):
            block = got_ref[b * count_z + c].astype(f32)
            for a in range(1, count_x):
                block = block + got_ref[a * each + b * count_z + c].astype(f32)
            stack.append(block)
        stack = jnp.concatenate(stack, axis=0)
        for h in range(pack):
            part = jnp.dot(stack, z_ref[c, h], precision=highest, preferred_element_type=f32)
            halves[h] = part if halves[h] is None else halves[h] + part
    lines = jnp.concatenate(halves, axis=0)
    wave = jnp.dot(y_ref[...], lines, precision=highest, preferred_element_type=f32)
    scaled = g_ref[...] * wave
    energy = jnp.sum(jnp.sum(scaled * wave, axis=1, keepdims=True), axis=0, keepdims=True)
    hi = energy.astype(bf16).astype(f32)
    mid = (energy - hi).astype(bf16).astype(f32)
    low = energy - hi - mid
    which = lax.broadcasted_iota(jnp.int32, (16, LANES), 0)
    tail = jnp.where(which == 0, hi, jnp.where(which == 1, mid, jnp.where(which == 2, low, 0.0)))
    back = lax.dot_general(y_ref[...], scaled, TN, precision=highest, preferred_element_type=f32)
    high = back.shape[0] // pack
    for c in range(count_z):
        total = None
        for h in range(pack):
            part = lax.dot_general(
                back[h * high : (h + 1) * high], z_ref[c, h], NT, precision=highest, preferred_element_type=f32
            )
            total = part if total is None else total + part
        for b in range(count_y):
            out_ref[b * count_z + c, 0:rows, :] = total[b * rows : (b + 1) * rows].astype(bf16)
            out_ref[b * count_z + c, rows : rows + 16, :] = tail.astype(bf16)


def mesh_kernel(
    counts, local, pack, owners, scale, escale,
    corner_ref, fraction_ref, charge_ref, wave_ref, z_ref, y_ref, g_ref,
    out_ref, energy_ref,
    hx_ref, left_ref, right_ref, payload_ref, got_ref, solved_ref, field_ref,
    send_one, recv_one, send_two, recv_two,
):
    local_x, local_y, local_z = local
    total = counts[0] * counts[1] * counts[2]
    each = counts[1] * counts[2]
    rows = payload_ref.shape[1]
    per = rows // local_y
    atoms = corner_ref.shape[-1]
    me = (lax.axis_index("gx") * counts[1] + lax.axis_index("gy")) * counts[2] + lax.axis_index("gz")
    barrier = pltpu.get_barrier_semaphore()

    def greet(k, carry):
        pl.semaphore_signal(
            barrier,
            inc=1,
            device_id=coordinates(lax.rem(me + k, total), counts),
            device_id_type=pl.DeviceIdType.MESH,
        )
        return carry

    lax.fori_loop(1, total, greet, 0)

    rows_x = spline(corner_ref[0:1, :], fraction_ref[0:1, :], local_x)
    rows_y = spline(corner_ref[1:2, :], fraction_ref[1:2, :], local_y)
    charged = rows_y * charge_ref[...]
    hx_ref[...] = jnp.dot(wave_ref[...], rows_x, precision=highest, preferred_element_type=f32)
    half = hx_ref.shape[0] // pack
    spread = None
    for h in range(pack):

        def fill(k, carry):
            left_ref[pl.ds(pl.multiple_of(k * local_y, local_y), local_y), :] = (
                hx_ref[pl.ds(h * half + k, 1), :] * charged
            ).astype(bf16)
            return carry

        lax.fori_loop(0, half, fill, 0, unroll=8)
        right = spline(corner_ref[2:3, :], fraction_ref[2:3, :], LANES, h * local_z).astype(bf16)
        right_ref[h] = right
        part = lax.dot_general(left_ref[...], right, NT, preferred_element_type=f32)
        spread = part if spread is None else spread + part
    payload_ref[...] = spread.astype(bf16).reshape(payload_ref.shape)
    got_ref[me] = payload_ref[jnp.minimum(me, owners - 1)]
    pl.semaphore_wait(barrier, total - 1)

    def guarded(fact, act):
        if owners == total:
            act()
        else:
            pl.when(fact)(act)

    def copy(k, source, target, send, recv):
        return pltpu.make_async_remote_copy(
            src_ref=source,
            dst_ref=target.at[me],
            send_sem=send.at[k],
            recv_sem=recv.at[k],
            device_id=coordinates(lax.rem(me + k, total), counts),
            device_id_type=pl.DeviceIdType.MESH,
        )

    def first(k):
        to = lax.rem(me + k, total)
        return to, copy(k, payload_ref.at[jnp.minimum(to, owners - 1)], got_ref, send_one, recv_one)

    def second(k):
        to = lax.rem(me + k, total)
        return to, copy(k, solved_ref.at[lax.rem(to, each)], field_ref, send_two, recv_two)

    def begin_one(k, carry):
        to, move = first(k)
        guarded(to < owners, lambda: move.start())
        return carry

    def arrive_one(k, carry):
        to, move = first(k)
        guarded(me < owners, lambda: move.wait_recv())
        return carry

    lax.fori_loop(1, total, begin_one, 0)
    lax.fori_loop(1, total, arrive_one, 0)
    solve_planes(counts, pack, got_ref, z_ref, y_ref, g_ref, solved_ref)

    def begin_two(k, carry):
        to, move = second(k)
        guarded(me < owners, lambda: move.start())
        return carry

    lax.fori_loop(1, total, begin_two, 0)
    field_ref[me] = solved_ref[lax.rem(me, each)]

    group = 4 if total % 4 == 0 else 1

    def gather(index, carry):
        acc, tail = carry
        sources, blocks = [], []
        for i in range(group):
            k = index * group + i
            source = lax.rem(me - k + total, total)

            def arrive(k=k):
                second(k)[1].wait_recv()

            if owners == total:
                pl.when(k > 0)(arrive)
            else:
                pl.when((k > 0) & (source < owners))(arrive)
            block = field_ref[source]
            if owners < total:
                block = jnp.where(source < owners, block.astype(f32), 0.0).astype(bf16)
            sources.append(jnp.minimum(source, owners - 1))
            blocks.append(block[0:rows])
            tail = tail + block[rows:].astype(f32)
        stack = jnp.concatenate(blocks, axis=0)
        for h in range(pack):
            value = jnp.dot(stack, right_ref[h], preferred_element_type=f32)
            for i, source in enumerate(sources):
                for k in range(per):
                    at = (i * per + k) * local_y
                    acc = acc + value[at : at + local_y] * hx_ref[
                        pl.ds(h * half + source * per + k, 1), :
                    ]
        return acc, tail

    acc, tail = lax.fori_loop(
        0, total // group, gather,
        (jnp.zeros((local_y, atoms), f32), jnp.zeros((16, LANES), f32)),
    )
    value = scale * jnp.sum(acc * rows_y, axis=0, keepdims=True)
    out_ref[...] = jnp.broadcast_to(value, out_ref.shape)
    energy_ref[...] = jnp.broadcast_to(escale * jnp.sum(tail, axis=0, keepdims=True), energy_ref.shape)

    def leave(k, carry):
        to, move = first(k)
        guarded(to < owners, lambda: move.wait_send())
        move_two = second(k)[1]
        guarded(me < owners, lambda: move_two.wait_send())
        return carry

    lax.fori_loop(1, total, leave, 0)


def influence_of(index_x, index_y, index_z, size_x, size_y, size_z, points):
    def wave(index, size):
        signed = jnp.where(2 * index >= size, index - size, index)
        return signed.astype(f32) * (points / size)

    wave_x = wave(index_x, size_x)
    wave_y = wave(index_y, size_y)
    wave_z = wave(index_z, size_z)
    squared = wave_x * wave_x + wave_y * wave_y + wave_z * wave_z
    safe = jnp.where(squared > 0, squared, 1.0)
    return jnp.where(squared > 0, jnp.exp(-((math.pi * spread_width) ** 2) * squared) / safe, 0.0)


def params(**kw):
    return pltpu.CompilerParams(vmem_limit_bytes=48 * 1024 * 1024, **kw)


def body(features, msg_weight, self_weight, charge_weight, spline_corner, spline_fraction):
    cells = features.shape[:3]
    slots, width = features.shape[3:]
    number = cells[0] * cells[1] * cells[2]
    counts = tuple(lax.axis_size(a) for a in AXES)
    devices = counts[0] * counts[1] * counts[2]
    local = tuple(c * PC for c in cells)
    size = tuple(c * n for c, n in zip(local, counts))
    pack = LANES // local[2]
    planes = max(pack, size[0] // devices)
    owners = size[0] // planes
    inner = planes // pack
    rows = inner * local[1]
    atoms = number * slots
    volume = size[0] // PC * (size[1] // PC) * (size[2] // PC)

    flat = features.reshape(number * slots, width)
    projected = jnp.dot(flat, msg_weight, preferred_element_type=f32).astype(bf16).reshape(features.shape)
    position = lax.reduce_precision(
        (spline_corner.astype(f32) + 1.0 + spline_fraction) / PC, 8, 7
    )
    norm = jnp.sum(position * position, axis=3, keepdims=True)
    one = jnp.ones_like(norm)
    near = jnp.concatenate(
        [position, one, one, one, one, one, one, *split3(-norm), position, one], axis=3
    ).astype(bf16)
    centre = jnp.concatenate(
        [2.0 * position, *split3(1.0 - norm), position] + [one] * 7, axis=3
    ).astype(bf16).reshape(number, 16, slots)
    table = offset_table()

    padded = exchange_halo(jnp.concatenate([projected, near], axis=3), 0, counts)
    values = padded[:, :, :, :slots]
    nears = padded[:, :, :, slots:]

    read = jnp.broadcast_to(charge_weight.astype(f32)[None, :], (8, width))
    cell_features = features.reshape(number, slots, width)
    square = (number, slots, width)
    preact, charge = pl.pallas_call(
        functools.partial(message_kernel, cells, counts),
        out_shape=(jax.ShapeDtypeStruct(square, f32), jax.ShapeDtypeStruct((number, 8, slots), f32)),
        grid=(number,),
        in_specs=[
            cell_spec(centre.shape),
            full_spec(table.shape),
            full_spec(nears.shape),
            full_spec(values.shape),
            cell_spec(square),
            full_spec(self_weight.shape),
            full_spec(read.shape),
        ],
        out_specs=(cell_spec(square), cell_spec((number, 8, slots))),
        compiler_params=params(),
        name="message",
    )(centre, table, nears, values, cell_features, self_weight, read)

    shift = jnp.stack(
        [lax.broadcasted_iota(jnp.int32, cells + (slots,), d) * PC for d in range(3)], axis=0
    )
    corner = (spline_corner.transpose(3, 0, 1, 2, 4) + shift).reshape(3, atoms)
    fraction = spline_fraction.transpose(3, 0, 1, 2, 4).reshape(3, atoms)
    order = (
        jnp.arange(pack, dtype=jnp.int32)[:, None, None] * inner
        + jnp.arange(owners, dtype=jnp.int32)[None, :, None] * planes
        + jnp.arange(inner, dtype=jnp.int32)[None, None, :]
    ).reshape(-1)
    here = lax.axis_index("gx") * local[0] + jnp.arange(local[0], dtype=jnp.int32)
    wave_x = cas(order, here, size[0])
    charges = charge[:, 0, :].reshape(1, atoms)
    range_y = jnp.arange(size[1], dtype=jnp.int32)
    range_z = jnp.arange(size[2], dtype=jnp.int32)
    cas_z = cas(range_z, range_z, size[2]).reshape(counts[2], 1, local[2], size[2])
    blank = jnp.zeros_like(cas_z)
    wide_z = jnp.concatenate(
        [
            jnp.concatenate([cas_z if at == h else blank for at in range(pack)], axis=2)
            for h in range(pack)
        ],
        axis=1,
    )
    cas_y = cas(range_y, range_y, size[1]).reshape(size[1], counts[1], local[1])
    same = jnp.eye(planes, dtype=f32).reshape(pack, inner, pack, inner)
    wide_y = jnp.einsum("abcd,kgy->abkcgdy", same, cas_y, precision=highest).reshape(
        planes * size[1], planes * size[1]
    )
    me = lax.axis_index(AXES)
    index_x = me * planes + jnp.arange(planes, dtype=jnp.int32)
    influence = influence_of(
        index_x[:, None, None], range_y[None, :, None], range_z[None, None, :], *size, PC
    ).reshape(planes * size[1], size[2])
    each = counts[1] * counts[2]
    potential, energy = pl.pallas_call(
        functools.partial(
            mesh_kernel,
            counts,
            local,
            pack,
            owners,
            coupling / volume,
            coupling / (2.0 * volume * atoms * devices),
        ),
        out_shape=(jax.ShapeDtypeStruct((8, atoms), f32), jax.ShapeDtypeStruct((8, LANES), f32)),
        scratch_shapes=[
            pltpu.VMEM((size[0], atoms), f32),
            pltpu.VMEM((owners * rows, atoms), bf16),
            pltpu.VMEM((pack, LANES, atoms), bf16),
            pltpu.VMEM((owners, rows, LANES), bf16),
            pltpu.VMEM((devices, rows, LANES), bf16),
            pltpu.VMEM((each, rows + 16, LANES), bf16),
            pltpu.VMEM((devices, rows + 16, LANES), bf16),
        ]
        + [pltpu.SemaphoreType.DMA((devices,))] * 4,
        compiler_params=params(collective_id=2, has_side_effects=True),
        name="mesh",
    )(corner, fraction, charges, wave_x, wide_z, wide_y, influence)
    potential = potential[0].reshape(cells + (slots,))

    pre = preact.reshape(features.shape)
    sigma = jax.nn.sigmoid(pre)
    slope = sigma * (1.0 + pre * (1.0 - sigma))
    cotangent = (potential[..., None] * charge_weight.astype(f32) * slope).astype(bf16)
    cots = exchange_halo(cotangent, 1, counts)
    grad = pl.pallas_call(
        functools.partial(back_kernel, cells, counts),
        out_shape=jax.ShapeDtypeStruct(square, f32),
        grid=(number,),
        in_specs=[
            cell_spec(centre.shape),
            full_spec(table.shape),
            full_spec(nears.shape),
            full_spec(cots.shape),
            cell_spec(square),
            full_spec(msg_weight.shape),
            full_spec(self_weight.shape),
        ],
        out_specs=cell_spec(square),
        compiler_params=params(),
        name="back",
    )(centre, table, nears, cots, cotangent.reshape(square), msg_weight, self_weight)
    return (grad.reshape(features.shape), potential, energy[0, 0])


def solution(mesh):
    split = P("gx", "gy", "gz", None, None)
    in_specs = (split, P(), P(), P(), split, split)
    out_specs = (split, P("gx", "gy", "gz", None), P())
    return jax.shard_map(body, mesh=mesh, in_specs=in_specs, out_specs=out_specs, check_vma=False)
```

```python
import functools
import math

import jax
import jax.numpy as jnp
from jax import lax
from jax.experimental import pallas as pl
from jax.experimental.pallas import tpu as pltpu
from jax.sharding import PartitionSpec as P

PC = 16
LANES = 128
pair_scale = 0.1
coupling = 0.125
spread_width = 0.0625
highest = lax.Precision.HIGHEST
AXES = ("gx", "gy", "gz")
f32 = jnp.float32
bf16 = jnp.bfloat16
NT = (((1,), (1,)), ((), ()))
TN = (((0,), (0,)), ((), ()))


def split3(value):
    hi = lax.reduce_precision(value, 8, 7)
    rest = value - hi
    mid = lax.reduce_precision(rest, 8, 7)
    return hi, mid, rest - mid


def cas(first, second, length):
    angle = 2.0 * math.pi / length * (first[:, None] * second[None, :] % length).astype(f32)
    return jnp.cos(angle) + jnp.sin(angle)


def offsets():
    return [(i, j, k) for i in (-1, 0, 1) for j in (-1, 0, 1) for k in (-1, 0, 1)]


def offset_table():
    rows = []
    for o in offsets():
        norm = float(o[0] ** 2 + o[1] ** 2 + o[2] ** 2)
        doubled = [2.0 * v for v in o]
        rows.append([1.0] * 6 + doubled + [1.0] * 3 + [-v for v in doubled] + [-norm])
    return jnp.broadcast_to(jnp.array(rows, f32)[:, :, None], (27, 16, LANES)).astype(bf16)


def slot(offset, devices, length):
    if devices == 2 and length == 1:
        return 0 if offset == 0 else 1
    return 1 + offset


def coordinates(index, counts):
    return (index // (counts[1] * counts[2]), index // counts[2] % counts[1], index % counts[2])


def halo_plan(counts, lengths):
    doubled = [n == 2 and length == 1 for n, length in zip(counts, lengths)]
    own = [(0, 1) if two else (1, 1 + length) for two, length in zip(doubled, lengths)]

    def faces(d):
        if doubled[d]:
            return {1: ((0, 1), (1, 2))}
        length = lengths[d]
        return {1: ((length, length + 1), (0, 1)), -1: ((1, 2), (length + 1, length + 2))}

    moves = []

    def add(d, way, source, target, need):
        moves.append((d, way, tuple(source), tuple(target), need))
        return len(moves) - 1

    lines = [(own[2], None)]
    for way, (source, target) in faces(2).items():
        lines.append(
            (target, add(2, way, (own[0], own[1], source), (own[0], own[1], target), None))
        )
    sheets = []
    for at_z, need_z in lines:
        sheets.append((own[1], at_z, need_z))
        for way, (source, target) in faces(1).items():
            need = add(1, way, (own[0], source, at_z), (own[0], target, at_z), need_z)
            sheets.append((target, at_z, need))
    for at_y, at_z, need in sheets:
        for way, (source, target) in faces(0).items():
            add(0, way, (source, at_y, at_z), (target, at_y, at_z), need)
    padded = tuple(length + (1 if two else 2) for two, length in zip(doubled, lengths))
    return padded, own, moves


def run_halo(counts, lengths, src_ref, out_ref, send_sem, recv_sem, own_sem, idle):
    padded, own, moves = halo_plan(counts, lengths)
    me = [lax.axis_index(a) for a in AXES]

    def neighbour(d, way):
        where = list(me)
        where[d] = lax.rem(me[d] + way + counts[d], counts[d])
        return tuple(where)

    barrier = pltpu.get_barrier_semaphore()
    links = sorted({(d, way) for d, way, *_ in moves})
    for d, way in links:
        pl.semaphore_signal(
            barrier, inc=1, device_id=neighbour(d, way), device_id_type=pl.DeviceIdType.MESH
        )
    pl.semaphore_wait(barrier, len(links))

    def region(ref, spans, shift=(0, 0, 0)):
        return ref.at[tuple(slice(lo - s, hi - s) for (lo, hi), s in zip(spans, shift))]

    starts = [lo for lo, _ in own]
    copies = []
    for which, (d, way, source, target, need) in enumerate(moves):
        origin = region(src_ref, source, starts) if need is None else region(out_ref, source)
        copies.append(
            pltpu.make_async_remote_copy(
                src_ref=origin,
                dst_ref=region(out_ref, target),
                send_sem=send_sem.at[which],
                recv_sem=recv_sem.at[which],
                device_id=neighbour(d, way),
                device_id_type=pl.DeviceIdType.MESH,
            )
        )
    keep = pltpu.make_async_copy(src_ref, region(out_ref, own), own_sem)
    ready = [w for w, m in enumerate(moves) if m[4] is None]
    for which in ready:
        copies[which].start()
    keep.start()
    idle()
    waited = set()

    def forward(which):
        copies[which].wait_recv()
        waited.add(which)
        for later, move in enumerate(moves):
            if move[4] == which:
                copies[later].start()

    for which, move in enumerate(moves):
        if which not in waited and any(m[4] == which for m in moves):
            forward(which)
    keep.wait()

    def arrive():
        for which in range(len(moves)):
            if which not in waited:
                copies[which].wait_recv()

    def leave():
        for copy in copies:
            copy.wait_send()

    return arrive, leave


def halo_scratch(shape, dtype, counts):
    padded, _, moves = halo_plan(counts, shape[:3])
    return [
        pltpu.VMEM(padded + shape[3:], dtype),
        pltpu.SemaphoreType.DMA((len(moves),)),
        pltpu.SemaphoreType.DMA((len(moves),)),
        pltpu.SemaphoreType.DMA,
    ]


def pair_part(cells, counts, centre_ref, table_ref, near_of, value_of, acc_ref, inner):
    plane = cells[1] * cells[2]
    for at_x in range(cells[0]):
        chosen = [
            (w, o) for w, o in enumerate(offsets()) if (0 <= at_x + o[0] < cells[0]) == inner
        ]
        if not chosen:
            continue

        def one(i, carry, at_x=at_x, chosen=chosen):
            base = (at_x, lax.div(i, cells[2]), lax.rem(i, cells[2]))
            cell = at_x * plane + i
            centre = centre_ref[cell]
            total = acc_ref[cell]
            for which, o in chosen:
                where = tuple(
                    start + slot(step, count, length)
                    for start, step, count, length in zip(base, o, counts, cells)
                )
                inside = lax.dot_general(
                    centre, near_of(where) * table_ref[which], TN, preferred_element_type=f32
                )
                inside = jnp.maximum(inside, 0.0)
                weight = (pair_scale * inside * inside).astype(bf16)
                total = total + jnp.dot(weight, value_of(where), preferred_element_type=f32)
            acc_ref[cell] = total
            return carry

        lax.fori_loop(0, plane, one, 0)


def message_kernel(
    cells, counts, slots, centre_ref, table_ref, src_ref, feature_ref, self_ref, read_ref,
    pre_ref, charge_ref, near_ref,
    pad_ref, send_sem, recv_sem, own_sem,
):
    number = cells[0] * cells[1] * cells[2]

    def begin():
        def one(i, carry):
            pre_ref[i] = jnp.dot(feature_ref[i], self_ref[...], preferred_element_type=f32)
            return carry

        lax.fori_loop(0, number, one, 0)

    arrive, leave = run_halo(counts, cells, src_ref, pad_ref, send_sem, recv_sem, own_sem, begin)

    def near_of(where):
        return pad_ref[where[0], where[1], where[2], slots:, :]

    def value_of(where):
        return pad_ref[where[0], where[1], where[2], :slots, :]

    pair_part(cells, counts, centre_ref, table_ref, near_of, value_of, pre_ref, True)
    arrive()
    pair_part(cells, counts, centre_ref, table_ref, near_of, value_of, pre_ref, False)

    def read(i, carry):
        preact = pre_ref[i]
        active = preact / (1.0 + jnp.exp(-preact))
        charge_ref[i] = lax.dot_general(
            read_ref[...], active, NT, precision=highest, preferred_element_type=f32
        )
        return carry

    lax.fori_loop(0, number, read, 0)
    near_ref[...] = pad_ref[:, :, :, slots:, :]
    leave()


def back_kernel(
    cells, counts, centre_ref, table_ref, near_ref, src_ref, cot_ref, msg_ref, self_ref,
    out_ref,
    pad_ref, acc_ref, send_sem, recv_sem, own_sem,
):
    number = cells[0] * cells[1] * cells[2]

    def begin():
        acc_ref[...] = jnp.zeros_like(acc_ref)

        def one(i, carry):
            out_ref[i] = lax.dot_general(
                cot_ref[i], self_ref[...], NT, preferred_element_type=f32
            )
            return carry

        lax.fori_loop(0, number, one, 0)

    arrive, leave = run_halo(counts, cells, src_ref, pad_ref, send_sem, recv_sem, own_sem, begin)

    def near_of(where):
        return near_ref[where[0], where[1], where[2]]

    def value_of(where):
        return pad_ref[where[0], where[1], where[2]]

    pair_part(cells, counts, centre_ref, table_ref, near_of, value_of, acc_ref, True)
    arrive()
    pair_part(cells, counts, centre_ref, table_ref, near_of, value_of, acc_ref, False)

    def one(i, carry):
        out_ref[i] = out_ref[i] + lax.dot_general(
            acc_ref[i].astype(bf16), msg_ref[...], NT, preferred_element_type=f32
        )
        return carry

    lax.fori_loop(0, number, one, 0)
    leave()


def spline(corner, fraction, points, start=0):
    atoms = corner.shape[-1]
    offset = lax.broadcasted_iota(jnp.int32, (points, atoms), 0) - start - corner
    u = fraction
    first = (1.0 - u) * (1.0 - u) * (1.0 - u) / 6.0
    second = (3.0 * u * u * u - 6.0 * u * u + 4.0) / 6.0
    third = (-3.0 * u * u * u + 3.0 * u * u + 3.0 * u + 1.0) / 6.0
    fourth = u * u * u / 6.0
    zero = jnp.zeros((points, atoms), f32)
    return jnp.where(
        offset == 0,
        first,
        jnp.where(offset == 1, second, jnp.where(offset == 2, third, jnp.where(offset == 3, fourth, zero))),
    )


def solve_planes(counts, pack, got_ref, z_ref, y_ref, g_ref, out_ref):
    count_x, count_y, count_z = counts
    rows = got_ref.shape[1]
    each = count_y * count_z
    halves = [None] * pack
    for c in range(count_z):
        stack = []
        for b in range(count_y):
            block = got_ref[b * count_z + c].astype(f32)
            for a in range(1, count_x):
                block = block + got_ref[a * each + b * count_z + c].astype(f32)
            stack.append(block)
        stack = jnp.concatenate(stack, axis=0)
        for h in range(pack):
            part = jnp.dot(stack, z_ref[c, h], precision=highest, preferred_element_type=f32)
            halves[h] = part if halves[h] is None else halves[h] + part
    lines = jnp.concatenate(halves, axis=0)
    wave = jnp.dot(y_ref[...], lines, precision=highest, preferred_element_type=f32)
    scaled = g_ref[...] * wave
    energy = jnp.sum(jnp.sum(scaled * wave, axis=1, keepdims=True), axis=0, keepdims=True)
    hi = energy.astype(bf16).astype(f32)
    mid = (energy - hi).astype(bf16).astype(f32)
    low = energy - hi - mid
    which = lax.broadcasted_iota(jnp.int32, (16, LANES), 0)
    tail = jnp.where(which == 0, hi, jnp.where(which == 1, mid, jnp.where(which == 2, low, 0.0)))
    back = lax.dot_general(y_ref[...], scaled, TN, precision=highest, preferred_element_type=f32)
    high = back.shape[0] // pack
    for c in range(count_z):
        total = None
        for h in range(pack):
            part = lax.dot_general(
                back[h * high : (h + 1) * high], z_ref[c, h], NT, precision=highest, preferred_element_type=f32
            )
            total = part if total is None else total + part
        for b in range(count_y):
            out_ref[b * count_z + c, 0:rows, :] = total[b * rows : (b + 1) * rows].astype(bf16)
            out_ref[b * count_z + c, rows : rows + 16, :] = tail.astype(bf16)


def mesh_kernel(
    counts, local, pack, owners, scale, escale,
    corner_ref, fraction_ref, charge_ref, wave_ref, z_ref, y_ref, g_ref,
    out_ref, energy_ref,
    hx_ref, left_ref, right_ref, payload_ref, got_ref, solved_ref, field_ref,
    send_one, recv_one, send_two, recv_two,
):
    local_x, local_y, local_z = local
    total = counts[0] * counts[1] * counts[2]
    each = counts[1] * counts[2]
    rows = payload_ref.shape[1]
    per = rows // local_y
    atoms = corner_ref.shape[-1]
    me = (lax.axis_index("gx") * counts[1] + lax.axis_index("gy")) * counts[2] + lax.axis_index("gz")
    barrier = pltpu.get_barrier_semaphore()

    def greet(k, carry):
        pl.semaphore_signal(
            barrier,
            inc=1,
            device_id=coordinates(lax.rem(me + k, total), counts),
            device_id_type=pl.DeviceIdType.MESH,
        )
        return carry

    lax.fori_loop(1, total, greet, 0)

    rows_x = spline(corner_ref[0:1, :], fraction_ref[0:1, :], local_x)
    rows_y = spline(corner_ref[1:2, :], fraction_ref[1:2, :], local_y)
    charged = rows_y * charge_ref[...]
    hx_ref[...] = jnp.dot(wave_ref[...], rows_x, precision=highest, preferred_element_type=f32)
    half = hx_ref.shape[0] // pack
    spread = None
    for h in range(pack):

        def fill(k, carry):
            left_ref[pl.ds(pl.multiple_of(k * local_y, local_y), local_y), :] = (
                hx_ref[pl.ds(h * half + k, 1), :] * charged
            ).astype(bf16)
            return carry

        lax.fori_loop(0, half, fill, 0, unroll=8)
        right = spline(corner_ref[2:3, :], fraction_ref[2:3, :], LANES, h * local_z).astype(bf16)
        right_ref[h] = right
        part = lax.dot_general(left_ref[...], right, NT, preferred_element_type=f32)
        spread = part if spread is None else spread + part
    payload_ref[...] = spread.astype(bf16).reshape(payload_ref.shape)
    got_ref[me] = payload_ref[jnp.minimum(me, owners - 1)]
    pl.semaphore_wait(barrier, total - 1)

    def guarded(fact, act):
        if owners == total:
            act()
        else:
            pl.when(fact)(act)

    def copy(k, source, target, send, recv):
        return pltpu.make_async_remote_copy(
            src_ref=source,
            dst_ref=target.at[me],
            send_sem=send.at[k],
            recv_sem=recv.at[k],
            device_id=coordinates(lax.rem(me + k, total), counts),
            device_id_type=pl.DeviceIdType.MESH,
        )

    def first(k):
        to = lax.rem(me + k, total)
        return to, copy(k, payload_ref.at[jnp.minimum(to, owners - 1)], got_ref, send_one, recv_one)

    def second(k):
        to = lax.rem(me + k, total)
        return to, copy(k, solved_ref.at[lax.rem(to, each)], field_ref, send_two, recv_two)

    def begin_one(k, carry):
        to, move = first(k)
        guarded(to < owners, lambda: move.start())
        return carry

    def arrive_one(k, carry):
        to, move = first(k)
        guarded(me < owners, lambda: move.wait_recv())
        return carry

    lax.fori_loop(1, total, begin_one, 0)
    lax.fori_loop(1, total, arrive_one, 0)
    solve_planes(counts, pack, got_ref, z_ref, y_ref, g_ref, solved_ref)

    def begin_two(k, carry):
        to, move = second(k)
        guarded(me < owners, lambda: move.start())
        return carry

    lax.fori_loop(1, total, begin_two, 0)
    field_ref[me] = solved_ref[lax.rem(me, each)]

    group = 4 if total % 4 == 0 else 1

    def gather(index, carry):
        acc, tail = carry
        sources, blocks = [], []
        for i in range(group):
            k = index * group + i
            source = lax.rem(me - k + total, total)

            def arrive(k=k):
                second(k)[1].wait_recv()

            if owners == total:
                pl.when(k > 0)(arrive)
            else:
                pl.when((k > 0) & (source < owners))(arrive)
            block = field_ref[source]
            if owners < total:
                block = jnp.where(source < owners, block.astype(f32), 0.0).astype(bf16)
            sources.append(jnp.minimum(source, owners - 1))
            blocks.append(block[0:rows])
            tail = tail + block[rows:].astype(f32)
        stack = jnp.concatenate(blocks, axis=0)
        for h in range(pack):
            value = jnp.dot(stack, right_ref[h], preferred_element_type=f32)
            for i, source in enumerate(sources):
                for k in range(per):
                    at = (i * per + k) * local_y
                    acc = acc + value[at : at + local_y] * hx_ref[
                        pl.ds(h * half + source * per + k, 1), :
                    ]
        return acc, tail

    acc, tail = lax.fori_loop(
        0, total // group, gather,
        (jnp.zeros((local_y, atoms), f32), jnp.zeros((16, LANES), f32)),
    )
    value = scale * jnp.sum(acc * rows_y, axis=0, keepdims=True)
    out_ref[...] = jnp.broadcast_to(value, out_ref.shape)
    energy_ref[...] = jnp.broadcast_to(escale * jnp.sum(tail, axis=0, keepdims=True), energy_ref.shape)

    def leave(k, carry):
        to, move = first(k)
        guarded(to < owners, lambda: move.wait_send())
        move_two = second(k)[1]
        guarded(me < owners, lambda: move_two.wait_send())
        return carry

    lax.fori_loop(1, total, leave, 0)


def influence_of(index_x, index_y, index_z, size_x, size_y, size_z, points):
    def wave(index, size):
        signed = jnp.where(2 * index >= size, index - size, index)
        return signed.astype(f32) * (points / size)

    wave_x = wave(index_x, size_x)
    wave_y = wave(index_y, size_y)
    wave_z = wave(index_z, size_z)
    squared = wave_x * wave_x + wave_y * wave_y + wave_z * wave_z
    safe = jnp.where(squared > 0, squared, 1.0)
    return jnp.where(squared > 0, jnp.exp(-((math.pi * spread_width) ** 2) * squared) / safe, 0.0)


def params(**kw):
    return pltpu.CompilerParams(vmem_limit_bytes=48 * 1024 * 1024, **kw)


def body(features, msg_weight, self_weight, charge_weight, spline_corner, spline_fraction):
    cells = features.shape[:3]
    slots, width = features.shape[3:]
    number = cells[0] * cells[1] * cells[2]
    counts = tuple(lax.axis_size(a) for a in AXES)
    devices = counts[0] * counts[1] * counts[2]
    local = tuple(c * PC for c in cells)
    size = tuple(c * n for c, n in zip(local, counts))
    pack = LANES // local[2]
    planes = max(pack, size[0] // devices)
    owners = size[0] // planes
    inner = planes // pack
    rows = inner * local[1]
    atoms = number * slots
    volume = size[0] // PC * (size[1] // PC) * (size[2] // PC)

    flat = features.reshape(number * slots, width)
    projected = jnp.dot(flat, msg_weight, preferred_element_type=f32).astype(bf16).reshape(features.shape)
    position = lax.reduce_precision(
        (spline_corner.astype(f32) + 1.0 + spline_fraction) / PC, 8, 7
    )
    norm = jnp.sum(position * position, axis=3, keepdims=True)
    one = jnp.ones_like(norm)
    near = jnp.concatenate(
        [position, one, one, one, one, one, one, *split3(-norm), position, one], axis=3
    ).astype(bf16)
    centre = jnp.concatenate(
        [2.0 * position, *split3(1.0 - norm), position] + [one] * 7, axis=3
    ).astype(bf16).reshape(number, 16, slots)
    table = offset_table()

    source = jnp.concatenate([projected, near], axis=3)
    padded = halo_plan(counts, cells)[0]

    read = jnp.broadcast_to(charge_weight.astype(f32)[None, :], (8, width))
    cell_features = features.reshape(number, slots, width)
    square = (number, slots, width)
    preact, charge, nears = pl.pallas_call(
        functools.partial(message_kernel, cells, counts, slots),
        out_shape=(
            jax.ShapeDtypeStruct(square, f32),
            jax.ShapeDtypeStruct((number, 8, slots), f32),
            jax.ShapeDtypeStruct(padded + near.shape[3:], bf16),
        ),
        scratch_shapes=halo_scratch(source.shape, bf16, counts),
        compiler_params=params(collective_id=0, has_side_effects=True),
        name="message",
    )(centre, table, source, cell_features, self_weight, read)

    shift = jnp.stack(
        [lax.broadcasted_iota(jnp.int32, cells + (slots,), d) * PC for d in range(3)], axis=0
    )
    corner = (spline_corner.transpose(3, 0, 1, 2, 4) + shift).reshape(3, atoms)
    fraction = spline_fraction.transpose(3, 0, 1, 2, 4).reshape(3, atoms)
    order = (
        jnp.arange(pack, dtype=jnp.int32)[:, None, None] * inner
        + jnp.arange(owners, dtype=jnp.int32)[None, :, None] * planes
        + jnp.arange(inner, dtype=jnp.int32)[None, None, :]
    ).reshape(-1)
    here = lax.axis_index("gx") * local[0] + jnp.arange(local[0], dtype=jnp.int32)
    wave_x = cas(order, here, size[0])
    charges = charge[:, 0, :].reshape(1, atoms)
    range_y = jnp.arange(size[1], dtype=jnp.int32)
    range_z = jnp.arange(size[2], dtype=jnp.int32)
    cas_z = cas(range_z, range_z, size[2]).reshape(counts[2], 1, local[2], size[2])
    blank = jnp.zeros_like(cas_z)
    wide_z = jnp.concatenate(
        [
            jnp.concatenate([cas_z if at == h else blank for at in range(pack)], axis=2)
            for h in range(pack)
        ],
        axis=1,
    )
    cas_y = cas(range_y, range_y, size[1]).reshape(size[1], counts[1], local[1])
    same = jnp.eye(planes, dtype=f32).reshape(pack, inner, pack, inner)
    wide_y = jnp.einsum("abcd,kgy->abkcgdy", same, cas_y, precision=highest).reshape(
        planes * size[1], planes * size[1]
    )
    me = lax.axis_index(AXES)
    index_x = me * planes + jnp.arange(planes, dtype=jnp.int32)
    influence = influence_of(
        index_x[:, None, None], range_y[None, :, None], range_z[None, None, :], *size, PC
    ).reshape(planes * size[1], size[2])
    each = counts[1] * counts[2]
    potential, energy = pl.pallas_call(
        functools.partial(
            mesh_kernel,
            counts,
            local,
            pack,
            owners,
            coupling / volume,
            coupling / (2.0 * volume * atoms * devices),
        ),
        out_shape=(jax.ShapeDtypeStruct((8, atoms), f32), jax.ShapeDtypeStruct((8, LANES), f32)),
        scratch_shapes=[
            pltpu.VMEM((size[0], atoms), f32),
            pltpu.VMEM((owners * rows, atoms), bf16),
            pltpu.VMEM((pack, LANES, atoms), bf16),
            pltpu.VMEM((owners, rows, LANES), bf16),
            pltpu.VMEM((devices, rows, LANES), bf16),
            pltpu.VMEM((each, rows + 16, LANES), bf16),
            pltpu.VMEM((devices, rows + 16, LANES), bf16),
        ]
        + [pltpu.SemaphoreType.DMA((devices,))] * 4,
        compiler_params=params(collective_id=2, has_side_effects=True),
        name="mesh",
    )(corner, fraction, charges, wave_x, wide_z, wide_y, influence)
    potential = potential[0].reshape(cells + (slots,))

    pre = preact.reshape(features.shape)
    sigma = jax.nn.sigmoid(pre)
    slope = sigma * (1.0 + pre * (1.0 - sigma))
    cotangent = (potential[..., None] * charge_weight.astype(f32) * slope).astype(bf16)
    scratch = halo_scratch(cotangent.shape, bf16, counts)
    grad = pl.pallas_call(
        functools.partial(back_kernel, cells, counts),
        out_shape=jax.ShapeDtypeStruct(square, f32),
        scratch_shapes=scratch[:1] + [pltpu.VMEM(square, f32)] + scratch[1:],
        compiler_params=params(collective_id=1, has_side_effects=True),
        name="back",
    )(centre, table, nears, cotangent, cotangent.reshape(square), msg_weight, self_weight)
    return (grad.reshape(features.shape), potential, energy[0, 0])


def solution(mesh):
    split = P("gx", "gy", "gz", None, None)
    in_specs = (split, P(), P(), P(), split, split)
    out_specs = (split, P("gx", "gy", "gz", None), P())
    return jax.shard_map(body, mesh=mesh, in_specs=in_specs, out_specs=out_specs, check_vma=False)
```

```python
import functools
import math

import jax
import jax.numpy as jnp
import numpy as np
from jax import lax
from jax.experimental import pallas as pl
from jax.experimental.pallas import tpu as pltpu
from jax.sharding import PartitionSpec as P

PC = 16
LANES = 128
pair_scale = 0.1
coupling = 0.125
spread_width = 0.0625
highest = lax.Precision.HIGHEST
AXES = ("gx", "gy", "gz")
f32 = jnp.float32
bf16 = jnp.bfloat16
NT = (((1,), (1,)), ((), ()))
TN = (((0,), (0,)), ((), ()))


def split3(value):
    hi = lax.reduce_precision(value, 8, 7)
    rest = value - hi
    mid = lax.reduce_precision(rest, 8, 7)
    return hi, mid, rest - mid


def cas(first, second, length):
    angle = 2.0 * np.pi / length * (first[:, None] * second[None, :] % length)
    return (np.cos(angle) + np.sin(angle)).astype(np.float32)


def offsets():
    return [(i, j, k) for i in (-1, 0, 1) for j in (-1, 0, 1) for k in (-1, 0, 1)]


def offset_table():
    rows = []
    for o in offsets():
        norm = float(o[0] ** 2 + o[1] ** 2 + o[2] ** 2)
        doubled = [2.0 * v for v in o]
        rows.append([1.0] * 6 + doubled + [1.0] * 3 + [-v for v in doubled] + [-norm])
    table = np.broadcast_to(np.array(rows, np.float32)[:, :, None], (27, 16, LANES))
    return jnp.asarray(table).astype(bf16)


def slot(offset, devices, length):
    if devices == 2 and length == 1:
        return 0 if offset == 0 else 1
    return 1 + offset


def coordinates(index, counts):
    return (index // (counts[1] * counts[2]), index // counts[2] % counts[1], index % counts[2])


def halo_plan(counts, lengths):
    doubled = [n == 2 and length == 1 for n, length in zip(counts, lengths)]
    own = [(0, 1) if two else (1, 1 + length) for two, length in zip(doubled, lengths)]

    def faces(d):
        if doubled[d]:
            return {1: ((0, 1), (1, 2))}
        length = lengths[d]
        return {1: ((length, length + 1), (0, 1)), -1: ((1, 2), (length + 1, length + 2))}

    moves = []

    def add(d, way, source, target, need):
        moves.append((d, way, tuple(source), tuple(target), need))
        return len(moves) - 1

    lines = [(own[2], None)]
    for way, (source, target) in faces(2).items():
        lines.append(
            (target, add(2, way, (own[0], own[1], source), (own[0], own[1], target), None))
        )
    sheets = []
    for at_z, need_z in lines:
        sheets.append((own[1], at_z, need_z))
        for way, (source, target) in faces(1).items():
            need = add(1, way, (own[0], source, at_z), (own[0], target, at_z), need_z)
            sheets.append((target, at_z, need))
    for at_y, at_z, need in sheets:
        for way, (source, target) in faces(0).items():
            add(0, way, (source, at_y, at_z), (target, at_y, at_z), need)
    padded = tuple(length + (1 if two else 2) for two, length in zip(doubled, lengths))
    return padded, own, moves


def run_halo(counts, lengths, src_ref, out_ref, send_sem, recv_sem, own_sem, idle):
    padded, own, moves = halo_plan(counts, lengths)
    me = [lax.axis_index(a) for a in AXES]

    def neighbour(d, way):
        where = list(me)
        where[d] = lax.rem(me[d] + way + counts[d], counts[d])
        return tuple(where)

    barrier = pltpu.get_barrier_semaphore()
    links = sorted({(d, way) for d, way, *_ in moves})
    for d, way in links:
        pl.semaphore_signal(
            barrier, inc=1, device_id=neighbour(d, way), device_id_type=pl.DeviceIdType.MESH
        )
    pl.semaphore_wait(barrier, len(links))

    def region(ref, spans, shift=(0, 0, 0)):
        return ref.at[tuple(slice(lo - s, hi - s) for (lo, hi), s in zip(spans, shift))]

    starts = [lo for lo, _ in own]
    copies = []
    for which, (d, way, source, target, need) in enumerate(moves):
        origin = region(src_ref, source, starts) if need is None else region(out_ref, source)
        copies.append(
            pltpu.make_async_remote_copy(
                src_ref=origin,
                dst_ref=region(out_ref, target),
                send_sem=send_sem.at[which],
                recv_sem=recv_sem.at[which],
                device_id=neighbour(d, way),
                device_id_type=pl.DeviceIdType.MESH,
            )
        )
    keep = pltpu.make_async_copy(src_ref, region(out_ref, own), own_sem)
    ready = [w for w, m in enumerate(moves) if m[4] is None]
    for which in ready:
        copies[which].start()
    keep.start()
    idle()
    waited = set()

    def forward(which):
        copies[which].wait_recv()
        waited.add(which)
        for later, move in enumerate(moves):
            if move[4] == which:
                copies[later].start()

    for which, move in enumerate(moves):
        if which not in waited and any(m[4] == which for m in moves):
            forward(which)
    keep.wait()

    def arrive():
        for which in range(len(moves)):
            if which not in waited:
                copies[which].wait_recv()

    def leave():
        for copy in copies:
            copy.wait_send()

    return arrive, leave


def halo_scratch(shape, dtype, counts):
    padded, _, moves = halo_plan(counts, shape[:3])
    return [
        pltpu.VMEM(padded + shape[3:], dtype),
        pltpu.SemaphoreType.DMA((len(moves),)),
        pltpu.SemaphoreType.DMA((len(moves),)),
        pltpu.SemaphoreType.DMA,
    ]


def pair_part(cells, counts, centre_ref, table_ref, near_of, value_of, acc_ref, inner):
    plane = cells[1] * cells[2]
    for at_x in range(cells[0]):
        chosen = [
            (w, o) for w, o in enumerate(offsets()) if (0 <= at_x + o[0] < cells[0]) == inner
        ]
        if not chosen:
            continue

        def one(i, carry, at_x=at_x, chosen=chosen):
            base = (at_x, lax.div(i, cells[2]), lax.rem(i, cells[2]))
            cell = at_x * plane + i
            centre = centre_ref[cell]
            total = acc_ref[cell]
            for which, o in chosen:
                where = tuple(
                    start + slot(step, count, length)
                    for start, step, count, length in zip(base, o, counts, cells)
                )
                inside = lax.dot_general(
                    centre, near_of(where) * table_ref[which], TN, preferred_element_type=f32
                )
                inside = jnp.maximum(inside, 0.0)
                weight = (pair_scale * inside * inside).astype(bf16)
                total = total + jnp.dot(weight, value_of(where), preferred_element_type=f32)
            acc_ref[cell] = total
            return carry

        lax.fori_loop(0, plane, one, 0, unroll=4)


def message_kernel(
    cells, counts, slots, centre_ref, table_ref, src_ref, feature_ref, self_ref, read_ref,
    pre_ref, charge_ref, near_ref,
    pad_ref, send_sem, recv_sem, own_sem,
):
    number = cells[0] * cells[1] * cells[2]

    def begin():
        def one(i, carry):
            pre_ref[i] = jnp.dot(feature_ref[i], self_ref[...], preferred_element_type=f32)
            return carry

        lax.fori_loop(0, number, one, 0, unroll=4)

    arrive, leave = run_halo(counts, cells, src_ref, pad_ref, send_sem, recv_sem, own_sem, begin)

    def near_of(where):
        return pad_ref[where[0], where[1], where[2], slots:, :]

    def value_of(where):
        return pad_ref[where[0], where[1], where[2], :slots, :]

    pair_part(cells, counts, centre_ref, table_ref, near_of, value_of, pre_ref, True)
    arrive()
    pair_part(cells, counts, centre_ref, table_ref, near_of, value_of, pre_ref, False)

    def read(i, carry):
        preact = pre_ref[i]
        active = preact / (1.0 + jnp.exp(-preact))
        charge_ref[i] = lax.dot_general(
            read_ref[...], active, NT, precision=highest, preferred_element_type=f32
        )
        return carry

    lax.fori_loop(0, number, read, 0, unroll=4)
    near_ref[...] = pad_ref[:, :, :, slots:, :]
    leave()


def back_kernel(
    cells, counts, centre_ref, table_ref, near_ref, src_ref, cot_ref, msg_ref, self_ref,
    out_ref,
    pad_ref, acc_ref, send_sem, recv_sem, own_sem,
):
    number = cells[0] * cells[1] * cells[2]

    def begin():
        acc_ref[...] = jnp.zeros_like(acc_ref)

        def one(i, carry):
            out_ref[i] = lax.dot_general(
                cot_ref[i], self_ref[...], NT, preferred_element_type=f32
            )
            return carry

        lax.fori_loop(0, number, one, 0, unroll=4)

    arrive, leave = run_halo(counts, cells, src_ref, pad_ref, send_sem, recv_sem, own_sem, begin)

    def near_of(where):
        return near_ref[where[0], where[1], where[2]]

    def value_of(where):
        return pad_ref[where[0], where[1], where[2]]

    pair_part(cells, counts, centre_ref, table_ref, near_of, value_of, acc_ref, True)
    arrive()
    pair_part(cells, counts, centre_ref, table_ref, near_of, value_of, acc_ref, False)

    def one(i, carry):
        out_ref[i] = out_ref[i] + lax.dot_general(
            acc_ref[i].astype(bf16), msg_ref[...], NT, preferred_element_type=f32
        )
        return carry

    lax.fori_loop(0, number, one, 0, unroll=4)
    leave()


def spline(corner, fraction, points, start=0):
    atoms = corner.shape[-1]
    offset = lax.broadcasted_iota(jnp.int32, (points, atoms), 0) - start - corner
    u = fraction
    first = (1.0 - u) * (1.0 - u) * (1.0 - u) / 6.0
    second = (3.0 * u * u * u - 6.0 * u * u + 4.0) / 6.0
    third = (-3.0 * u * u * u + 3.0 * u * u + 3.0 * u + 1.0) / 6.0
    fourth = u * u * u / 6.0
    zero = jnp.zeros((points, atoms), f32)
    return jnp.where(
        offset == 0,
        first,
        jnp.where(offset == 1, second, jnp.where(offset == 2, third, jnp.where(offset == 3, fourth, zero))),
    )


def solve_planes(counts, pack, got_ref, z_ref, y_ref, g_ref, out_ref):
    count_x, count_y, count_z = counts
    rows = got_ref.shape[1]
    each = count_y * count_z
    halves = [None] * pack
    for c in range(count_z):
        stack = []
        for b in range(count_y):
            block = got_ref[b * count_z + c].astype(f32)
            for a in range(1, count_x):
                block = block + got_ref[a * each + b * count_z + c].astype(f32)
            stack.append(block)
        stack = jnp.concatenate(stack, axis=0)
        for h in range(pack):
            part = jnp.dot(stack, z_ref[c, h], precision=highest, preferred_element_type=f32)
            halves[h] = part if halves[h] is None else halves[h] + part
    lines = jnp.concatenate(halves, axis=0)
    wave = jnp.dot(y_ref[...], lines, precision=highest, preferred_element_type=f32)
    scaled = g_ref[...] * wave
    energy = jnp.sum(jnp.sum(scaled * wave, axis=1, keepdims=True), axis=0, keepdims=True)
    hi = energy.astype(bf16).astype(f32)
    mid = (energy - hi).astype(bf16).astype(f32)
    low = energy - hi - mid
    which = lax.broadcasted_iota(jnp.int32, (16, LANES), 0)
    tail = jnp.where(which == 0, hi, jnp.where(which == 1, mid, jnp.where(which == 2, low, 0.0)))
    back = lax.dot_general(y_ref[...], scaled, TN, precision=highest, preferred_element_type=f32)
    high = back.shape[0] // pack
    for c in range(count_z):
        total = None
        for h in range(pack):
            part = lax.dot_general(
                back[h * high : (h + 1) * high], z_ref[c, h], NT, precision=highest, preferred_element_type=f32
            )
            total = part if total is None else total + part
        for b in range(count_y):
            out_ref[b * count_z + c, 0:rows, :] = total[b * rows : (b + 1) * rows].astype(bf16)
            out_ref[b * count_z + c, rows : rows + 16, :] = tail.astype(bf16)


def mesh_kernel(
    counts, local, pack, owners, scale, escale,
    corner_ref, fraction_ref, charge_ref, wave_ref, z_ref, y_ref, g_ref,
    out_ref, energy_ref,
    hx_ref, left_ref, right_ref, payload_ref, got_ref, solved_ref, field_ref,
    send_one, recv_one, send_two, recv_two,
):
    local_x, local_y, local_z = local
    total = counts[0] * counts[1] * counts[2]
    each = counts[1] * counts[2]
    rows = payload_ref.shape[1]
    per = rows // local_y
    atoms = corner_ref.shape[-1]
    me = (lax.axis_index("gx") * counts[1] + lax.axis_index("gy")) * counts[2] + lax.axis_index("gz")
    barrier = pltpu.get_barrier_semaphore()

    def greet(k, carry):
        pl.semaphore_signal(
            barrier,
            inc=1,
            device_id=coordinates(lax.rem(me + k, total), counts),
            device_id_type=pl.DeviceIdType.MESH,
        )
        return carry

    lax.fori_loop(1, total, greet, 0)

    rows_x = spline(corner_ref[0:1, :], fraction_ref[0:1, :], local_x)
    rows_y = spline(corner_ref[1:2, :], fraction_ref[1:2, :], local_y)
    charged = rows_y * charge_ref[...]
    hx_ref[...] = jnp.dot(wave_ref[...], rows_x, precision=highest, preferred_element_type=f32)
    half = hx_ref.shape[0] // pack
    spread = None
    for h in range(pack):

        def fill(k, carry):
            left_ref[pl.ds(pl.multiple_of(k * local_y, local_y), local_y), :] = (
                hx_ref[pl.ds(h * half + k, 1), :] * charged
            ).astype(bf16)
            return carry

        lax.fori_loop(0, half, fill, 0, unroll=8)
        right = spline(corner_ref[2:3, :], fraction_ref[2:3, :], LANES, h * local_z).astype(bf16)
        right_ref[h] = right
        part = lax.dot_general(left_ref[...], right, NT, preferred_element_type=f32)
        spread = part if spread is None else spread + part
    payload_ref[...] = spread.astype(bf16).reshape(payload_ref.shape)
    got_ref[me] = payload_ref[jnp.minimum(me, owners - 1)]
    pl.semaphore_wait(barrier, total - 1)

    def guarded(fact, act):
        if owners == total:
            act()
        else:
            pl.when(fact)(act)

    def copy(k, source, target, send, recv):
        return pltpu.make_async_remote_copy(
            src_ref=source,
            dst_ref=target.at[me],
            send_sem=send.at[k],
            recv_sem=recv.at[k],
            device_id=coordinates(lax.rem(me + k, total), counts),
            device_id_type=pl.DeviceIdType.MESH,
        )

    def first(k):
        to = lax.rem(me + k, total)
        return to, copy(k, payload_ref.at[jnp.minimum(to, owners - 1)], got_ref, send_one, recv_one)

    def second(k):
        to = lax.rem(me + k, total)
        return to, copy(k, solved_ref.at[lax.rem(to, each)], field_ref, send_two, recv_two)

    def begin_one(k, carry):
        to, move = first(k)
        guarded(to < owners, lambda: move.start())
        return carry

    def arrive_one(k, carry):
        to, move = first(k)
        guarded(me < owners, lambda: move.wait_recv())
        return carry

    lax.fori_loop(1, total, begin_one, 0)
    lax.fori_loop(1, total, arrive_one, 0)
    solve_planes(counts, pack, got_ref, z_ref, y_ref, g_ref, solved_ref)

    def begin_two(k, carry):
        to, move = second(k)
        guarded(me < owners, lambda: move.start())
        return carry

    lax.fori_loop(1, total, begin_two, 0)
    field_ref[me] = solved_ref[lax.rem(me, each)]

    group = 4 if total % 4 == 0 else 1

    def gather(index, carry):
        acc, tail = carry
        sources, blocks = [], []
        for i in range(group):
            k = index * group + i
            source = lax.rem(me - k + total, total)

            def arrive(k=k):
                second(k)[1].wait_recv()

            if owners == total:
                pl.when(k > 0)(arrive)
            else:
                pl.when((k > 0) & (source < owners))(arrive)
            block = field_ref[source]
            if owners < total:
                block = jnp.where(source < owners, block.astype(f32), 0.0).astype(bf16)
            sources.append(jnp.minimum(source, owners - 1))
            blocks.append(block[0:rows])
            tail = tail + block[rows:].astype(f32)
        stack = jnp.concatenate(blocks, axis=0)
        for h in range(pack):
            value = jnp.dot(stack, right_ref[h], preferred_element_type=f32)
            for i, source in enumerate(sources):
                for k in range(per):
                    at = (i * per + k) * local_y
                    acc = acc + value[at : at + local_y] * hx_ref[
                        pl.ds(h * half + source * per + k, 1), :
                    ]
        return acc, tail

    acc, tail = lax.fori_loop(
        0, total // group, gather,
        (jnp.zeros((local_y, atoms), f32), jnp.zeros((16, LANES), f32)),
    )
    value = scale * jnp.sum(acc * rows_y, axis=0, keepdims=True)
    out_ref[...] = jnp.broadcast_to(value, out_ref.shape)
    energy_ref[...] = jnp.broadcast_to(escale * jnp.sum(tail, axis=0, keepdims=True), energy_ref.shape)

    def leave(k, carry):
        to, move = first(k)
        guarded(to < owners, lambda: move.wait_send())
        move_two = second(k)[1]
        guarded(me < owners, lambda: move_two.wait_send())
        return carry

    lax.fori_loop(1, total, leave, 0)


def influence_of(index_x, index_y, index_z, size_x, size_y, size_z, points):
    def wave(index, size):
        signed = jnp.where(2 * index >= size, index - size, index)
        return signed.astype(f32) * (points / size)

    wave_x = wave(index_x, size_x)
    wave_y = wave(index_y, size_y)
    wave_z = wave(index_z, size_z)
    squared = wave_x * wave_x + wave_y * wave_y + wave_z * wave_z
    safe = jnp.where(squared > 0, squared, 1.0)
    return jnp.where(squared > 0, jnp.exp(-((math.pi * spread_width) ** 2) * squared) / safe, 0.0)


def params(**kw):
    return pltpu.CompilerParams(vmem_limit_bytes=48 * 1024 * 1024, **kw)


def body(features, msg_weight, self_weight, charge_weight, spline_corner, spline_fraction):
    cells = features.shape[:3]
    slots, width = features.shape[3:]
    number = cells[0] * cells[1] * cells[2]
    counts = tuple(lax.axis_size(a) for a in AXES)
    devices = counts[0] * counts[1] * counts[2]
    local = tuple(c * PC for c in cells)
    size = tuple(c * n for c, n in zip(local, counts))
    pack = LANES // local[2]
    planes = max(pack, size[0] // devices)
    owners = size[0] // planes
    inner = planes // pack
    rows = inner * local[1]
    atoms = number * slots
    volume = size[0] // PC * (size[1] // PC) * (size[2] // PC)

    flat = features.reshape(number * slots, width)
    projected = jnp.dot(flat, msg_weight, preferred_element_type=f32).astype(bf16).reshape(features.shape)
    position = lax.reduce_precision(
        (spline_corner.astype(f32) + 1.0 + spline_fraction) / PC, 8, 7
    )
    norm = jnp.sum(position * position, axis=3, keepdims=True)
    one = jnp.ones_like(norm)
    near = jnp.concatenate(
        [position, one, one, one, one, one, one, *split3(-norm), position, one], axis=3
    ).astype(bf16)
    centre = jnp.concatenate(
        [2.0 * position, *split3(1.0 - norm), position] + [one] * 7, axis=3
    ).astype(bf16).reshape(number, 16, slots)
    table = offset_table()

    source = jnp.concatenate([projected, near], axis=3)
    padded = halo_plan(counts, cells)[0]

    read = jnp.broadcast_to(charge_weight.astype(f32)[None, :], (8, width))
    cell_features = features.reshape(number, slots, width)
    square = (number, slots, width)
    preact, charge, nears = pl.pallas_call(
        functools.partial(message_kernel, cells, counts, slots),
        out_shape=(
            jax.ShapeDtypeStruct(square, f32),
            jax.ShapeDtypeStruct((number, 8, slots), f32),
            jax.ShapeDtypeStruct(padded + near.shape[3:], bf16),
        ),
        scratch_shapes=halo_scratch(source.shape, bf16, counts),
        compiler_params=params(collective_id=0, has_side_effects=True),
        name="message",
    )(centre, table, source, cell_features, self_weight, read)

    shift = jnp.stack(
        [lax.broadcasted_iota(jnp.int32, cells + (slots,), d) * PC for d in range(3)], axis=0
    )
    corner = (spline_corner.transpose(3, 0, 1, 2, 4) + shift).reshape(3, atoms)
    fraction = spline_fraction.transpose(3, 0, 1, 2, 4).reshape(3, atoms)
    order = (
        np.arange(pack)[:, None, None] * inner
        + np.arange(owners)[None, :, None] * planes
        + np.arange(inner)[None, None, :]
    ).reshape(-1)
    waves = cas(np.arange(size[0]), order, size[0]).reshape(counts[0], local[0], size[0])
    wave_x = lax.dynamic_index_in_dim(
        jnp.asarray(waves.transpose(0, 2, 1)), lax.axis_index("gx"), 0, keepdims=False
    )
    charges = charge[:, 0, :].reshape(1, atoms)
    range_y = jnp.arange(size[1], dtype=jnp.int32)
    range_z = jnp.arange(size[2], dtype=jnp.int32)
    cas_z = cas(np.arange(size[2]), np.arange(size[2]), size[2])
    wide_z = np.zeros((counts[2], pack, pack, local[2], size[2]), np.float32)
    for h in range(pack):
        wide_z[:, h, h] = cas_z.reshape(counts[2], local[2], size[2])
    wide_z = jnp.asarray(wide_z.reshape(counts[2], pack, pack * local[2], size[2]))
    cas_y = cas(np.arange(size[1]), np.arange(size[1]), size[1]).reshape(size[1], counts[1], local[1])
    same = np.eye(planes, dtype=np.float32).reshape(pack, inner, pack, inner)
    wide_y = jnp.asarray(
        np.einsum("abcd,kgy->abkcgdy", same, cas_y).reshape(planes * size[1], planes * size[1])
    )
    me = lax.axis_index(AXES)
    index_x = me * planes + jnp.arange(planes, dtype=jnp.int32)
    influence = influence_of(
        index_x[:, None, None], range_y[None, :, None], range_z[None, None, :], *size, PC
    ).reshape(planes * size[1], size[2])
    each = counts[1] * counts[2]
    potential, energy = pl.pallas_call(
        functools.partial(
            mesh_kernel,
            counts,
            local,
            pack,
            owners,
            coupling / volume,
            coupling / (2.0 * volume * atoms * devices),
        ),
        out_shape=(jax.ShapeDtypeStruct((8, atoms), f32), jax.ShapeDtypeStruct((8, LANES), f32)),
        scratch_shapes=[
            pltpu.VMEM((size[0], atoms), f32),
            pltpu.VMEM((owners * rows, atoms), bf16),
            pltpu.VMEM((pack, LANES, atoms), bf16),
            pltpu.VMEM((owners, rows, LANES), bf16),
            pltpu.VMEM((devices, rows, LANES), bf16),
            pltpu.VMEM((each, rows + 16, LANES), bf16),
            pltpu.VMEM((devices, rows + 16, LANES), bf16),
        ]
        + [pltpu.SemaphoreType.DMA((devices,))] * 4,
        compiler_params=params(collective_id=2, has_side_effects=True),
        name="mesh",
    )(corner, fraction, charges, wave_x, wide_z, wide_y, influence)
    potential = potential[0].reshape(cells + (slots,))

    pre = preact.reshape(features.shape)
    sigma = jax.nn.sigmoid(pre)
    slope = sigma * (1.0 + pre * (1.0 - sigma))
    cotangent = (potential[..., None] * charge_weight.astype(f32) * slope).astype(bf16)
    scratch = halo_scratch(cotangent.shape, bf16, counts)
    grad = pl.pallas_call(
        functools.partial(back_kernel, cells, counts),
        out_shape=jax.ShapeDtypeStruct(square, f32),
        scratch_shapes=scratch[:1] + [pltpu.VMEM(square, f32)] + scratch[1:],
        compiler_params=params(collective_id=1, has_side_effects=True),
        name="back",
    )(centre, table, nears, cotangent, cotangent.reshape(square), msg_weight, self_weight)
    return (grad.reshape(features.shape), potential, energy[0, 0])


def solution(mesh):
    split = P("gx", "gy", "gz", None, None)
    in_specs = (split, P(), P(), P(), split, split)
    out_specs = (split, P("gx", "gy", "gz", None), P())
    return jax.shard_map(body, mesh=mesh, in_specs=in_specs, out_specs=out_specs, check_vma=False)
```
